512 devices in a mesh: row: 32 (over z, core), col: 16 (over y, x).
Axes of the slice: x: 4, y: 4, z: 16, core: 2. Of those that a mesh axis runs over, the one named last changes fastest.
Arguments:
- tokens: bfloat16 [512, 16384], P('col', 'row'), may hold values from -6 to 6
- query_weight: bfloat16 [16384, 8192], P('row', 'col'), may hold values from -0.09375 to 0.09375
- keyval_weight: bfloat16 [16384, 2048], P('row', 'col'), may hold values from -0.09375 to 0.09375
Outputs:
- query_proj: bfloat16 [512, 8192], P('row', 'col')
- query_code: bfloat16 [16384, 8192], P('row', 'col')
- query_scale: float32 [128, 64], P('row', 'col')
- keyval_code: bfloat16 [16384, 2048], P('row', 'col')
- keyval_scale: float32 [128, 16], P('row', 'col')
The draws below stay inside these ranges and needn't reach their ends.
All inputs are finite; a program needn't handle non-finite values. Where the reference program divides by a largest or mean magnitude, that divisor is 1e-20 or more.
Results may differ from the reference program's by a relative error of at most 0.0095.
Values may be sent and summed in bfloat16 or wider, within the bound.
No kernel may reach another device: no remote copies, remote signals or barrier semaphores. Data moves between devices by JAX's collectives and lax.ppermute only.
A program may use at most 64 MiB of HBM per device.

```python
import math
import jax
import jax.numpy as jnp
from jax import lax

D = 16384
BLOCK = 128
QSTEPS = 4
ROWS = 512
QD = 8192
KVD = 1024
N_ROW = 32


def with_spikes(result, key, source, target, shards_of, factor):
    owner, partner = [(jnp.arange(result.shape[position]) // (result.shape[position] // shards_of)).reshape([-1 if axis == position else 1 for axis in range(result.ndim)]) for position in (source, target)]
    chosen = jax.random.permutation(key, shards_of)[partner]
    strong = (owner == chosen) | (owner == (partner + shards_of // 2) % shards_of)
    return jnp.where(strong, factor * result, result)


def block_scale(own_key, extent, shards, smallest, largest):
    gain = 1.0
    for axis_at, shards_of in shards:
        draws = jax.random.uniform(jax.random.fold_in(jax.random.fold_in(own_key, 6), axis_at), (shards_of,), jnp.float32, smallest / len(shards), largest / len(shards))
        gain = gain * jnp.repeat(jnp.exp(draws), extent[axis_at] // shards_of).reshape((-1,) + (1,) * (len(extent) - 1 - axis_at))
    return gain


def heavy_noise(own_key, extent, scale, limit, pieces, heavy, held_as=jnp.bfloat16):
    result = scale * jax.random.normal(own_key, extent, jnp.float32)
    if pieces:
        result = result * block_scale(own_key, extent, pieces, -0.22, 0.18)
    return jnp.clip(with_spikes(result, jax.random.fold_in(own_key, 3), *heavy), -limit, limit).astype(held_as)


def setup_inputs(seed: int = 0) -> dict:
    keys = jax.random.split(jax.random.key(seed), 4)
    tokens = heavy_noise(keys[0], (ROWS, D), 1.0, 6.0, ((0, 16), (1, 32)), (0, 1, 32, 2.75))
    query_weight = heavy_noise(keys[1], (D, QD), D ** -0.5, 0.09375, ((0, 32), (1, 16)), (1, 0, 32, 2.75))
    keyval_weight = heavy_noise(keys[2], (D, 2 * KVD), D ** -0.5, 0.09375, ((0, 32), (1, 16)), (1, 0, 32, 2.75))
    return dict(tokens=tokens, query_weight=query_weight, keyval_weight=keyval_weight)


EPSILON = 1e-06
SOFTNESS = 0.9
TWO_PI = 2.0 * math.pi

def soften(argument):
    return argument - SOFTNESS * jnp.sin(TWO_PI * argument) / TWO_PI

def block_codes(weight, smooth):
    smoothed = weight.astype(jnp.float32) * smooth[:, None]
    height, breadth = smoothed.shape
    tile_view = smoothed.reshape(height // BLOCK, BLOCK, breadth // BLOCK, BLOCK)
    scales = (lax.optimization_barrier(jnp.max(jnp.abs(tile_view), axis=(1, 3))) + EPSILON) / QSTEPS
    encoded = soften(tile_view / scales[:, None, :, None]).reshape(height, breadth).astype(jnp.bfloat16)
    return (encoded, scales)

def reference(tokens, query_weight, keyval_weight):
    act_peak = lax.optimization_barrier(jnp.max(jnp.abs(tokens), axis=0)).astype(jnp.float32)
    weight_peak = jnp.maximum(lax.optimization_barrier(jnp.max(jnp.abs(query_weight), axis=1)), lax.optimization_barrier(jnp.max(jnp.abs(keyval_weight), axis=1))).astype(jnp.float32)
    smooth = jnp.sqrt((act_peak + EPSILON) / (weight_peak + EPSILON))
    query_code, query_scale = block_codes(query_weight, smooth)
    keyval_code, keyval_scale = block_codes(keyval_weight, smooth)
    x_smooth = tokens.astype(jnp.float32) / smooth[None, :]
    token_scale = ((lax.optimization_barrier(jnp.max(jnp.abs(x_smooth), axis=1)) + EPSILON) / QSTEPS).astype(jnp.bfloat16)
    scale_rows = token_scale.astype(jnp.float32)
    x_code = soften(x_smooth / scale_rows[:, None]).astype(jnp.bfloat16)
    column_scale = jnp.repeat(query_scale, BLOCK, axis=1)
    per_group = D // N_ROW // BLOCK
    row_total = x_code.shape[0]
    out_width = query_code.shape[1]

    def group_sum(group_index, summed):

        def add_block(block_index, running):
            block_pos = (group_index * per_group + block_index).astype(jnp.int32)
            code_block = lax.dynamic_slice_in_dim(x_code, block_pos * BLOCK, BLOCK, 1)
            weight_block = lax.dynamic_slice_in_dim(query_code, block_pos * BLOCK, BLOCK, 0)
            scale_row = lax.dynamic_slice_in_dim(column_scale, block_pos, 1, 0)
            product = jnp.dot(code_block, weight_block, preferred_element_type=jnp.float32)
            return running + product * scale_row
        running = lax.fori_loop(0, per_group, add_block, jnp.zeros((row_total, out_width), jnp.float32))
        return summed + running * scale_rows[:, None]
    summed = lax.fori_loop(0, N_ROW, group_sum, jnp.zeros((row_total, out_width), jnp.float32))
    query_proj = summed.astype(jnp.bfloat16)
    return (query_proj, query_code, query_scale, keyval_code, keyval_scale)
```

```python
import functools

import jax
import jax.numpy as jnp
from jax import lax
from jax.experimental import pallas as pl
from jax.experimental.pallas import tpu as pltpu
from jax.sharding import Mesh, PartitionSpec as P

BLOCK = 128
QSTEPS = 4
EPSILON = 1e-06
ROUNDER = 12582912.0
SINE = (
    0.8999999761581421,
    -5.921761989593506,
    11.689058303833008,
    -10.986687660217285,
    6.018372535705566,
    -2.1297717094421387,
    0.45832234621047974,
)
VMEM = pl.BlockSpec(memory_space=pltpu.VMEM)


def soften(value):
    offset = value - ((value + ROUNDER) - ROUNDER)
    square = offset * offset
    series = SINE[-1]
    for term in SINE[-2::-1]:
        series = series * square + term
    return value - offset * series


def across(column_major):
    return jnp.max(column_major.T, axis=0, keepdims=True)


def down(row):
    return jnp.broadcast_to(row, (BLOCK, BLOCK)).T


def peaks_kernel(tokens_ref, query_ref, keyval_ref, out_ref):
    depth = query_ref.shape[0]
    tokens = tokens_ref[...]
    rows = tokens.shape[0]
    peaks = []
    for base in range(0, depth, BLOCK):
        top = jnp.abs(keyval_ref[base : base + BLOCK, :])
        for left in range(0, query_ref.shape[1], BLOCK):
            top = jnp.maximum(top, jnp.abs(query_ref[base : base + BLOCK, left : left + BLOCK]))
        peaks.append(across(top.astype(jnp.float32)))
    peak = jnp.broadcast_to(jnp.concatenate(peaks, axis=1), (8, depth)).astype(jnp.bfloat16)
    for copy in range(out_ref.shape[0]):
        out_ref[copy, :rows, :] = tokens
        out_ref[copy, rows:, :] = peak


def smooth_kernel(gathered_ref, smooth_ref, out_ref):
    members, padded, depth = gathered_ref.shape
    rows = padded - 8
    act = jnp.abs(gathered_ref[0, :rows, :])
    weight = gathered_ref[0, rows:, :]
    for member in range(1, members):
        act = jnp.maximum(act, jnp.abs(gathered_ref[member, :rows, :]))
        weight = jnp.maximum(weight, gathered_ref[member, rows:, :])
    act_peak = jnp.max(act.astype(jnp.float32), axis=0, keepdims=True)
    weight_peak = jnp.max(weight.astype(jnp.float32), axis=0, keepdims=True)
    smooth = jnp.sqrt((act_peak + EPSILON) / (weight_peak + EPSILON))
    inverse = 1.0 / smooth
    smooth_ref[0:1, :] = smooth
    smooth_ref[1:2, :] = inverse
    per_block = BLOCK // rows
    lines = []
    for first in range(0, members, per_block):
        top = None
        for left in range(0, depth, BLOCK):
            piece = jnp.abs(gathered_ref[first : first + per_block, :rows, left : left + BLOCK])
            piece = piece.astype(jnp.float32).reshape(BLOCK, BLOCK) * inverse[:, left : left + BLOCK]
            top = piece if top is None else jnp.maximum(top, piece)
        lines.append(across(top))
    peak = jnp.concatenate(lines, axis=0)
    for copy in range(out_ref.shape[0]):
        out_ref[copy] = peak


def weights_kernel(query_ref, keyval_ref, smooth_ref, query_out, query_scale, keyval_out, keyval_scale):
    smooth = smooth_ref[0:1, :]
    for source, code_ref, scale_ref in (
        (query_ref, query_out, query_scale),
        (keyval_ref, keyval_out, keyval_scale),
    ):
        for row, base in enumerate(range(0, source.shape[0], BLOCK)):
            factor = down(smooth[:, base : base + BLOCK])
            for column, left in enumerate(range(0, source.shape[1], BLOCK)):
                block = source[base : base + BLOCK, left : left + BLOCK].astype(jnp.float32) * factor
                top = jnp.max(jnp.max(jnp.abs(block), axis=0, keepdims=True), axis=1, keepdims=True)
                scale = (top + EPSILON) / QSTEPS
                scale_ref[row : row + 1, column : column + 1] = scale
                code = soften(block * (1.0 / scale)).astype(jnp.bfloat16)
                code_ref[base : base + BLOCK, left : left + BLOCK] = code


def project_kernel(core_ref, gathered_ref, smooth_ref, peaks_ref, code_ref, scale_ref, send_ref, keep_ref):
    members, padded, depth = gathered_ref.shape
    rows = padded - 8
    half = rows // 2
    peak = peaks_ref[0]
    for member in range(1, peaks_ref.shape[0]):
        peak = jnp.maximum(peak, peaks_ref[member])
    scale = ((peak + EPSILON) / QSTEPS).astype(jnp.bfloat16).astype(jnp.float32)
    inverse = smooth_ref[1:2, :]
    per_block = BLOCK // rows
    core = core_ref[0]
    blocks = depth // BLOCK
    column_scale = []
    for a in range(blocks):
        column_scale.append(
            jnp.concatenate(
                [
                    jnp.broadcast_to(scale_ref[a : a + 1, c : c + 1], (1, BLOCK))
                    for c in range(scale_ref.shape[1])
                ],
                axis=1,
            )
        )
    for index, first in enumerate(range(0, members, per_block)):
        row_scale = down(scale[index : index + 1, :])
        row_inverse = 1.0 / row_scale
        total = None
        for a in range(blocks):
            left = a * BLOCK
            piece = gathered_ref[first : first + per_block, :rows, left : left + BLOCK]
            piece = piece.astype(jnp.float32).reshape(BLOCK, BLOCK)
            value = piece * inverse[:, left : left + BLOCK] * row_inverse
            code = soften(value).astype(jnp.bfloat16)
            product = jnp.dot(
                code, code_ref[left : left + BLOCK, :], preferred_element_type=jnp.float32
            )
            product = product * column_scale[a]
            total = product if total is None else total + product
        width = total.shape[1]
        total = jnp.concatenate(
            [total[:, c : c + BLOCK] * row_scale for c in range(0, width, BLOCK)], axis=1
        )
        total = total.reshape(per_block, 2, half, width)
        low, high = total[:, 0], total[:, 1]
        first_core = core == 0
        send_ref[first : first + per_block] = jnp.where(first_core, high, low)
        keep_ref[first : first + per_block] = jnp.where(first_core, low, high)


def join_kernel(keep_ref, other_ref, out_ref):
    out_ref[...] = (keep_ref[...] + other_ref[...]).astype(out_ref.dtype)


def sum_kernel(parts_ref, out_ref):
    total = parts_ref[0].astype(jnp.float32)
    for part in range(1, parts_ref.shape[0]):
        total = total + parts_ref[part].astype(jnp.float32)
    out_ref[...] = total.astype(out_ref.dtype)


def call(kernel, out_shape, args, flops=0, specs=None, name=None):
    outs = out_shape if isinstance(out_shape, (tuple, list)) else (out_shape,)
    moved = sum(a.size * a.dtype.itemsize for a in (*args, *outs))
    return pl.pallas_call(
        kernel,
        out_shape=out_shape,
        in_specs=specs or [VMEM] * len(args),
        out_specs=jax.tree.map(lambda _: VMEM, out_shape),
        cost_estimate=pl.CostEstimate(flops=flops, bytes_accessed=moved, transcendentals=0),
        name=name,
    )(*args)


def exchange(array, axes):
    return lax.all_to_all(array, axes, 0, 0, tiled=True)


def body(chips, columns, tokens, query_weight, keyval_weight):
    f32, bf16 = jnp.float32, jnp.bfloat16
    shape = jax.ShapeDtypeStruct
    rows, depth = tokens.shape
    width = query_weight.shape[1]
    send = call(
        peaks_kernel, shape((columns, rows + 8, depth), bf16), (tokens, query_weight, keyval_weight),
        name="peaks",
    )
    gathered = exchange(send, ("y", "x"))
    smooth, row_peaks = call(
        smooth_kernel,
        (shape((8, depth), f32), shape((2 * chips, depth // BLOCK, BLOCK), f32)),
        (gathered,),
        name="smooth",
    )
    peaks = exchange(row_peaks, ("z", "core"))
    query_code, query_scale, keyval_code, keyval_scale = call(
        weights_kernel,
        (
            shape(query_weight.shape, bf16),
            shape((depth // BLOCK, width // BLOCK), f32),
            shape(keyval_weight.shape, bf16),
            shape((depth // BLOCK, keyval_weight.shape[1] // BLOCK), f32),
        ),
        (query_weight, keyval_weight, smooth),
        flops=20 * (query_weight.size + keyval_weight.size),
        name="weights",
    )
    half = shape((columns, rows // 2, width), f32)
    core = lax.axis_index("core").astype(jnp.int32).reshape(1)
    to_other, kept = call(
        project_kernel,
        (half, half),
        (core, gathered, smooth, peaks, query_code, query_scale),
        specs=[pl.BlockSpec(memory_space=pltpu.SMEM)] + [VMEM] * 5,
        flops=2 * columns * rows * depth * width,
        name="project",
    )
    from_other = lax.ppermute(to_other, "core", [(0, 1), (1, 0)])
    joined = call(join_kernel, shape(half.shape, bf16), (kept, from_other), name="join")
    parts = exchange(joined, "z")
    query_proj = call(sum_kernel, shape((rows // 2, width), bf16), (parts,), name="sum")
    return (query_proj, query_code, query_scale, keyval_code, keyval_scale)


def solution(mesh):
    rows, columns = mesh.devices.shape
    chips = rows // 2
    side = int(round(columns**0.5))
    fine = Mesh(
        mesh.devices.reshape(chips, 2, columns // side, side), ("z", "core", "y", "x")
    )
    row, col = ("z", "core"), ("y", "x")
    return jax.shard_map(
        functools.partial(body, chips, columns),
        mesh=fine,
        in_specs=(P(col, row), P(row, col), P(row, col)),
        out_specs=(P(row, col),) * 5,
        check_vma=False,
    )
```

```python
import functools

import jax
import jax.numpy as jnp
from jax import lax
from jax.experimental import pallas as pl
from jax.experimental.pallas import tpu as pltpu
from jax.sharding import Mesh, PartitionSpec as P

BLOCK = 128
QSTEPS = 4
EPSILON = 1e-06
ROUNDER = 12582912.0
SINE = (
    0.8999999761581421,
    -5.921761989593506,
    11.689058303833008,
    -10.986687660217285,
    6.018372535705566,
    -2.1297717094421387,
    0.45832234621047974,
)
VMEM = pl.BlockSpec(memory_space=pltpu.VMEM)


def soften(value):
    offset = value - ((value + ROUNDER) - ROUNDER)
    square = offset * offset
    series = SINE[-1]
    for term in SINE[-2::-1]:
        series = series * square + term
    return value - offset * series


def across(column_major):
    return jnp.max(column_major.T, axis=0, keepdims=True)


def down(row):
    return jnp.broadcast_to(row, (BLOCK, BLOCK)).T


def peaks_kernel(tokens_ref, query_ref, keyval_ref, out_ref):
    depth = query_ref.shape[0]
    tokens = tokens_ref[...]
    rows = tokens.shape[0]
    peaks = []
    for base in range(0, depth, BLOCK):
        top = jnp.abs(keyval_ref[base : base + BLOCK, :])
        for left in range(0, query_ref.shape[1], BLOCK):
            top = jnp.maximum(top, jnp.abs(query_ref[base : base + BLOCK, left : left + BLOCK]))
        peaks.append(across(top.astype(jnp.float32)))
    peak = jnp.broadcast_to(jnp.concatenate(peaks, axis=1), (8, depth)).astype(jnp.bfloat16)
    for copy in range(out_ref.shape[0]):
        out_ref[copy, :rows, :] = tokens
        out_ref[copy, rows:, :] = peak


def smooth_kernel(gathered_ref, smooth_ref, out_ref):
    members, padded, depth = gathered_ref.shape
    rows = padded - 8
    act = jnp.abs(gathered_ref[0, :rows, :])
    weight = gathered_ref[0, rows:, :]
    for member in range(1, members):
        act = jnp.maximum(act, jnp.abs(gathered_ref[member, :rows, :]))
        weight = jnp.maximum(weight, gathered_ref[member, rows:, :])
    act_peak = jnp.max(act.astype(jnp.float32), axis=0, keepdims=True)
    weight_peak = jnp.max(weight.astype(jnp.float32), axis=0, keepdims=True)
    smooth = jnp.sqrt((act_peak + EPSILON) / (weight_peak + EPSILON))
    inverse = 1.0 / smooth
    smooth_ref[0:1, :] = smooth
    smooth_ref[1:2, :] = inverse
    per_block = BLOCK // rows
    lines = []
    for first in range(0, members, per_block):
        top = None
        for left in range(0, depth, BLOCK):
            piece = jnp.abs(gathered_ref[first : first + per_block, :rows, left : left + BLOCK])
            piece = piece.astype(jnp.float32).reshape(BLOCK, BLOCK) * inverse[:, left : left + BLOCK]
            top = piece if top is None else jnp.maximum(top, piece)
        lines.append(across(top))
    peak = jnp.concatenate(lines, axis=0)
    for copy in range(out_ref.shape[0]):
        out_ref[copy] = peak


def weights_kernel(query_ref, keyval_ref, smooth_ref, query_out, query_scale, keyval_out, keyval_scale):
    smooth = smooth_ref[0:1, :]
    for source, code_ref, scale_ref in (
        (query_ref, query_out, query_scale),
        (keyval_ref, keyval_out, keyval_scale),
    ):
        for row, base in enumerate(range(0, source.shape[0], BLOCK)):
            factor = down(smooth[:, base : base + BLOCK])
            for column, left in enumerate(range(0, source.shape[1], BLOCK)):
                block = source[base : base + BLOCK, left : left + BLOCK].astype(jnp.float32) * factor
                top = jnp.max(jnp.max(jnp.abs(block), axis=0, keepdims=True), axis=1, keepdims=True)
                scale = (top + EPSILON) / QSTEPS
                scale_ref[row : row + 1, column : column + 1] = scale
                code = soften(block * (1.0 / scale)).astype(jnp.bfloat16)
                code_ref[base : base + BLOCK, left : left + BLOCK] = code


def project_kernel(core_ref, gathered_ref, smooth_ref, peaks_ref, code_ref, scale_ref, send_ref, keep_ref):
    members, padded, depth = gathered_ref.shape
    rows = padded - 8
    half = rows // 2
    peak = peaks_ref[0]
    for member in range(1, peaks_ref.shape[0]):
        peak = jnp.maximum(peak, peaks_ref[member])
    scale = ((peak + EPSILON) / QSTEPS).astype(jnp.bfloat16).astype(jnp.float32)
    inverse = smooth_ref[1:2, :]
    per_block = BLOCK // rows
    core = core_ref[0]
    blocks = depth // BLOCK
    column_scale = []
    for a in range(blocks):
        column_scale.append(
            jnp.concatenate(
                [
                    jnp.broadcast_to(scale_ref[a : a + 1, c : c + 1], (1, BLOCK))
                    for c in range(scale_ref.shape[1])
                ],
                axis=1,
            )
        )
    for index, first in enumerate(range(0, members, per_block)):
        row_scale = down(scale[index : index + 1, :])
        row_inverse = 1.0 / row_scale
        total = None
        for a in range(blocks):
            left = a * BLOCK
            piece = gathered_ref[first : first + per_block, :rows, left : left + BLOCK]
            piece = piece.astype(jnp.float32).reshape(BLOCK, BLOCK)
            value = piece * inverse[:, left : left + BLOCK] * row_inverse
            code = soften(value).astype(jnp.bfloat16)
            product = jnp.dot(
                code, code_ref[left : left + BLOCK, :], preferred_element_type=jnp.float32
            )
            product = product * column_scale[a]
            total = product if total is None else total + product
        width = total.shape[1]
        total = jnp.concatenate(
            [total[:, c : c + BLOCK] * row_scale for c in range(0, width, BLOCK)], axis=1
        )
        total = total.reshape(per_block, 2, half, width)
        low, high = total[:, 0], total[:, 1]
        first_core = core == 0
        send_ref[first : first + per_block] = jnp.where(first_core, high, low)
        keep_ref[first : first + per_block] = jnp.where(first_core, low, high)


def join_kernel(keep_ref, other_ref, out_ref):
    out_ref[...] = (keep_ref[...] + other_ref[...]).astype(out_ref.dtype)


def sum_kernel(parts_ref, out_ref):
    total = parts_ref[0].astype(jnp.float32)
    for part in range(1, parts_ref.shape[0]):
        total = total + parts_ref[part].astype(jnp.float32)
    out_ref[...] = total.astype(out_ref.dtype)


def call(kernel, out_shape, args, flops=0, specs=None, name=None):
    outs = out_shape if isinstance(out_shape, (tuple, list)) else (out_shape,)
    moved = sum(a.size * a.dtype.itemsize for a in (*args, *outs))
    return pl.pallas_call(
        kernel,
        out_shape=out_shape,
        in_specs=specs or [VMEM] * len(args),
        out_specs=jax.tree.map(lambda _: VMEM, out_shape),
        cost_estimate=pl.CostEstimate(flops=flops, bytes_accessed=moved, transcendentals=0),
        compiler_params=pltpu.CompilerParams(vmem_limit_bytes=8 << 20),
        name=name,
    )(*args)


def exchange(array, axes):
    return lax.all_to_all(array, axes, 0, 0, tiled=True)


def body(chips, columns, tokens, query_weight, keyval_weight):
    f32, bf16 = jnp.float32, jnp.bfloat16
    shape = jax.ShapeDtypeStruct
    rows, depth = tokens.shape
    width = query_weight.shape[1]
    send = call(
        peaks_kernel, shape((columns, rows + 8, depth), bf16), (tokens, query_weight, keyval_weight),
        name="peaks",
    )
    gathered = exchange(send, ("y", "x"))
    smooth, row_peaks = call(
        smooth_kernel,
        (shape((8, depth), f32), shape((2 * chips, depth // BLOCK, BLOCK), f32)),
        (gathered,),
        name="smooth",
    )
    peaks = exchange(row_peaks, ("z", "core"))
    query_code, query_scale, keyval_code, keyval_scale = call(
        weights_kernel,
        (
            shape(query_weight.shape, bf16),
            shape((depth // BLOCK, width // BLOCK), f32),
            shape(keyval_weight.shape, bf16),
            shape((depth // BLOCK, keyval_weight.shape[1] // BLOCK), f32),
        ),
        (query_weight, keyval_weight, smooth),
        flops=20 * (query_weight.size + keyval_weight.size),
        name="weights",
    )
    half = shape((columns, rows // 2, width), f32)
    core = lax.axis_index("core").astype(jnp.int32).reshape(1)
    to_other, kept = call(
        project_kernel,
        (half, half),
        (core, gathered, smooth, peaks, query_code, query_scale),
        specs=[pl.BlockSpec(memory_space=pltpu.SMEM)] + [VMEM] * 5,
        flops=2 * columns * rows * depth * width,
        name="project",
    )
    from_other = lax.ppermute(to_other, "core", [(0, 1), (1, 0)])
    joined = call(join_kernel, shape(half.shape, bf16), (kept, from_other), name="join")
    parts = exchange(joined, "z")
    query_proj = call(sum_kernel, shape((rows // 2, width), bf16), (parts,), name="sum")
    return (query_proj, query_code, query_scale, keyval_code, keyval_scale)


def solution(mesh):
    rows, columns = mesh.devices.shape
    chips = rows // 2
    side = int(round(columns**0.5))
    fine = Mesh(
        mesh.devices.reshape(chips, 2, columns // side, side), ("z", "core", "y", "x")
    )
    row, col = ("z", "core"), ("y", "x")
    return jax.shard_map(
        functools.partial(body, chips, columns),
        mesh=fine,
        in_specs=(P(col, row), P(row, col), P(row, col)),
        out_specs=(P(row, col),) * 5,
        check_vma=False,
    )
```

```python
import functools

import jax
import jax.numpy as jnp
from jax import lax
from jax.experimental import pallas as pl
from jax.experimental.pallas import tpu as pltpu
from jax.sharding import Mesh, PartitionSpec as P

BLOCK = 128
QSTEPS = 4
EPSILON = 1e-06
ROUNDER = 12582912.0
SINE = (
    0.8999999761581421,
    -5.921761989593506,
    11.689058303833008,
    -10.986687660217285,
    6.018372535705566,
    -2.1297717094421387,
    0.45832234621047974,
)
VMEM = pl.BlockSpec(memory_space=pltpu.VMEM)
SMEM = pl.BlockSpec(memory_space=pltpu.SMEM)
HBM = pl.BlockSpec(memory_space=pltpu.HBM)


def soften(value):
    offset = value - ((value + ROUNDER) - ROUNDER)
    square = offset * offset
    series = SINE[-1]
    for term in SINE[-2::-1]:
        series = series * square + term
    return value - offset * series


def across(column_major):
    return jnp.max(column_major.T, axis=0, keepdims=True)


def down(row):
    return jnp.broadcast_to(row, (BLOCK, BLOCK)).T


def peaks_kernel(tokens_hbm, query_hbm, keyval_hbm, out_ref, tokens_ref, query_ref, keyval_ref, sems):
    copies = [
        pltpu.make_async_copy(source, target, sems.at[index])
        for index, (source, target) in enumerate(
            ((query_hbm, query_ref), (keyval_hbm, keyval_ref), (tokens_hbm, tokens_ref))
        )
    ]
    for copy in copies:
        copy.start()
    for copy in copies:
        copy.wait()
    depth = query_ref.shape[0]
    half = tokens_ref.shape[0] // 2
    act = jnp.max(jnp.abs(tokens_ref[...]).astype(jnp.float32), axis=0, keepdims=True)
    peaks = []
    for base in range(0, depth, BLOCK):
        top = jnp.abs(keyval_ref[base : base + BLOCK, :])
        for left in range(0, query_ref.shape[1], BLOCK):
            top = jnp.maximum(top, jnp.abs(query_ref[base : base + BLOCK, left : left + BLOCK]))
        peaks.append(across(top.astype(jnp.float32)))
    weight = jnp.concatenate(peaks, axis=1)
    both = jnp.concatenate(
        [jnp.broadcast_to(act, (4, depth)), jnp.broadcast_to(weight, (4, depth))], axis=0
    ).astype(jnp.bfloat16)
    peers = out_ref.shape[0] // 2
    for core in range(2):
        rows = tokens_ref[core * half : (core + 1) * half, :]
        for peer in range(peers):
            out_ref[core * peers + peer, :half, :] = rows
            out_ref[core * peers + peer, half:, :] = both


def smooth_kernel(gathered_ref, smooth_ref, out_ref):
    members, padded, depth = gathered_ref.shape
    half = padded - 8
    peers = members // 2
    inverses = []
    for core in range(2):
        both = gathered_ref[core * peers, half:, :]
        for peer in range(1, peers):
            both = jnp.maximum(both, gathered_ref[core * peers + peer, half:, :])
        both = both.astype(jnp.float32)
        smooth = jnp.sqrt((both[0:1] + EPSILON) / (both[4:5] + EPSILON))
        smooth_ref[core, 0:1, :] = smooth
        smooth_ref[core, 1:2, :] = 1.0 / smooth
        inverses.append(1.0 / smooth)
    per_block = BLOCK // half
    lines = []
    for first in range(0, peers, per_block):
        top = None
        for core in range(2):
            start = core * peers + first
            for left in range(0, depth, BLOCK):
                piece = jnp.abs(gathered_ref[start : start + per_block, :half, left : left + BLOCK])
                piece = piece.astype(jnp.float32).reshape(BLOCK, BLOCK)
                piece = piece * inverses[core][:, left : left + BLOCK]
                top = piece if top is None else jnp.maximum(top, piece)
        lines.append(across(top))
    peak = jnp.concatenate(lines, axis=0)
    for copy in range(out_ref.shape[0]):
        out_ref[copy] = peak


def weights_kernel(
    core_ref, query_ref, keyval_ref, smooth_ref, send_ref, query_out, query_scale, keyval_out, keyval_scale
):
    smooth = smooth_ref[core_ref[0]][0:1, :]
    depth = query_ref.shape[0]
    lines = []
    for source, code_ref, scale_ref in (
        (query_ref, query_out, query_scale),
        (keyval_ref, keyval_out, keyval_scale),
    ):
        for row, base in enumerate(range(0, depth, BLOCK)):
            factor = down(smooth[:, base : base + BLOCK])
            scales = []
            for column, left in enumerate(range(0, source.shape[1], BLOCK)):
                block = source[base : base + BLOCK, left : left + BLOCK].astype(jnp.float32) * factor
                top = jnp.max(jnp.max(jnp.abs(block), axis=0, keepdims=True), axis=1, keepdims=True)
                scale = (top + EPSILON) / QSTEPS
                scale_ref[row : row + 1, column : column + 1] = scale
                scales.append(jnp.broadcast_to(scale, (1, BLOCK)))
                code = soften(block * (1.0 / scale)).astype(jnp.bfloat16)
                code_ref[base : base + BLOCK, left : left + BLOCK] = code
                if source is query_ref:
                    send_ref[base : base + BLOCK, left : left + BLOCK] = code
            if source is query_ref:
                lines.append(jnp.concatenate(scales, axis=1))
    rest = jnp.concatenate(lines, axis=0)
    pieces = []
    for _ in range(3):
        piece = rest.astype(jnp.bfloat16).astype(jnp.float32)
        rest = rest - piece
        pieces.append(piece)
    pieces.append(jnp.zeros_like(rest))
    send_ref[depth:, :] = jnp.concatenate(pieces, axis=0).astype(jnp.bfloat16)


def project_kernel(core_ref, gathered_ref, smooth_ref, peaks_ref, mine_ref, other_ref, out_ref):
    members, padded, depth = gathered_ref.shape
    half = padded - 8
    peers = members // 2
    peak = peaks_ref[0]
    for member in range(1, peaks_ref.shape[0]):
        peak = jnp.maximum(peak, peaks_ref[member])
    scale = ((peak + EPSILON) / QSTEPS).astype(jnp.bfloat16).astype(jnp.float32)
    per_block = BLOCK // half
    blocks = depth // BLOCK
    sides = []
    for core, code_ref in ((core_ref[0], mine_ref), (1 - core_ref[0], other_ref)):
        pieces = code_ref[depth:, :].astype(jnp.float32)
        column_scale = pieces[0:blocks] + pieces[blocks : 2 * blocks] + pieces[2 * blocks : 3 * blocks]
        sides.append((core * peers, smooth_ref[core][1:2, :], code_ref, column_scale))
    for index, first in enumerate(range(0, peers, per_block)):
        row_scale = down(scale[index : index + 1, :])
        row_inverse = 1.0 / row_scale
        total = None
        for start, inverse, code_ref, column_scale in sides:
            for a in range(blocks):
                left = a * BLOCK
                piece = gathered_ref[pl.ds(start + first, per_block), :half, left : left + BLOCK]
                piece = piece.astype(jnp.float32).reshape(BLOCK, BLOCK)
                value = piece * inverse[:, left : left + BLOCK] * row_inverse
                code = soften(value).astype(jnp.bfloat16)
                product = jnp.dot(
                    code, code_ref[left : left + BLOCK, :], preferred_element_type=jnp.float32
                )
                product = product * column_scale[a : a + 1]
                total = product if total is None else total + product
        width = total.shape[1]
        total = jnp.concatenate(
            [total[:, c : c + BLOCK] * row_scale for c in range(0, width, BLOCK)], axis=1
        )
        out_ref[first : first + per_block] = total.astype(out_ref.dtype).reshape(per_block, half, width)


def sum_kernel(parts_ref, out_ref):
    total = parts_ref[0].astype(jnp.float32)
    for part in range(1, parts_ref.shape[0]):
        total = total + parts_ref[part].astype(jnp.float32)
    out_ref[...] = total.astype(out_ref.dtype)


def call(kernel, out_shape, args, flops=0, specs=None, scratch=(), name=None):
    outs = out_shape if isinstance(out_shape, (tuple, list)) else (out_shape,)
    moved = sum(a.size * a.dtype.itemsize for a in (*args, *outs))
    return pl.pallas_call(
        kernel,
        out_shape=out_shape,
        in_specs=specs or [VMEM] * len(args),
        out_specs=jax.tree.map(lambda _: VMEM, out_shape),
        scratch_shapes=scratch,
        cost_estimate=pl.CostEstimate(flops=flops, bytes_accessed=moved, transcendentals=0),
        compiler_params=pltpu.CompilerParams(vmem_limit_bytes=8 << 20),
        name=name,
    )(*args)


def exchange(array, axes):
    return lax.all_to_all(array, axes, 0, 0, tiled=True)


def body(chips, columns, tokens, query_weight, keyval_weight):
    f32, bf16 = jnp.float32, jnp.bfloat16
    shape = jax.ShapeDtypeStruct
    rows, depth = tokens.shape
    half = rows // 2
    width = query_weight.shape[1]
    blocks = depth // BLOCK
    arguments = (tokens, query_weight, keyval_weight)
    send = call(
        peaks_kernel,
        shape((2 * columns, half + 8, depth), bf16),
        arguments,
        specs=[HBM] * 3,
        scratch=[pltpu.VMEM(a.shape, a.dtype) for a in arguments] + [pltpu.SemaphoreType.DMA((3,))],
        name="peaks",
    )
    gathered = exchange(send, ("core", "y", "x"))
    smooth, row_peaks = call(
        smooth_kernel,
        (shape((2, 8, depth), f32), shape((chips, columns * half // BLOCK, BLOCK), f32)),
        (gathered,),
        name="smooth",
    )
    peaks = exchange(row_peaks, "z")
    core = lax.axis_index("core").astype(jnp.int32).reshape(1)
    mine, query_code, query_scale, keyval_code, keyval_scale = call(
        weights_kernel,
        (
            shape((depth + 4 * blocks, width), bf16),
            shape(query_weight.shape, bf16),
            shape((blocks, width // BLOCK), f32),
            shape(keyval_weight.shape, bf16),
            shape((blocks, keyval_weight.shape[1] // BLOCK), f32),
        ),
        (core, query_weight, keyval_weight, smooth),
        specs=[SMEM] + [VMEM] * 3,
        flops=20 * (query_weight.size + keyval_weight.size),
        name="weights",
    )
    other = lax.ppermute(mine, "core", [(0, 1), (1, 0)])
    partial = call(
        project_kernel,
        shape((chips, half, width), bf16),
        (core, gathered, smooth, peaks, mine, other),
        specs=[SMEM] + [VMEM] * 5,
        flops=2 * columns * rows * depth * width,
        name="project",
    )
    parts = exchange(partial, "z")
    query_proj = call(sum_kernel, shape((half, width), bf16), (parts,), name="sum")
    return (query_proj, query_code, query_scale, keyval_code, keyval_scale)


def solution(mesh):
    rows, columns = mesh.devices.shape
    chips = rows // 2
    side = int(round(columns**0.5))
    fine = Mesh(
        mesh.devices.reshape(chips, 2, columns // side, side), ("z", "core", "y", "x")
    )
    row, col = ("z", "core"), ("y", "x")
    return jax.shard_map(
        functools.partial(body, chips, columns),
        mesh=fine,
        in_specs=(P(col, row), P(row, col), P(row, col)),
        out_specs=(P(row, col),) * 5,
        check_vma=False,
    )
```

```python
import functools

import jax
import jax.numpy as jnp
from jax import lax
from jax.experimental import pallas as pl
from jax.experimental.pallas import tpu as pltpu
from jax.sharding import Mesh, PartitionSpec as P

BLOCK = 128
QSTEPS = 4
EPSILON = 1e-06
ROUNDER = 12582912.0
SINE = (
    0.8999999761581421,
    -5.921761989593506,
    11.689058303833008,
    -10.986687660217285,
    6.018372535705566,
    -2.1297717094421387,
    0.45832234621047974,
)
VMEM = pl.BlockSpec(memory_space=pltpu.VMEM)
SMEM = pl.BlockSpec(memory_space=pltpu.SMEM)
HBM = pl.BlockSpec(memory_space=pltpu.HBM)


def soften(value):
    offset = value - ((value + ROUNDER) - ROUNDER)
    square = offset * offset
    series = SINE[-1]
    for term in SINE[-2::-1]:
        series = series * square + term
    return value - offset * series


def across(column_major):
    return jnp.max(column_major.T, axis=0, keepdims=True)


def down(row):
    return jnp.broadcast_to(row, (BLOCK, BLOCK)).T


def peaks_kernel(tokens_hbm, query_hbm, keyval_hbm, out_ref, tokens_ref, query_ref, keyval_ref, sems):
    copies = [
        pltpu.make_async_copy(source, target, sems.at[index])
        for index, (source, target) in enumerate(
            ((query_hbm, query_ref), (keyval_hbm, keyval_ref), (tokens_hbm, tokens_ref))
        )
    ]
    for copy in copies:
        copy.start()
    for copy in copies:
        copy.wait()
    depth = query_ref.shape[0]
    half = tokens_ref.shape[0] // 2
    act = jnp.max(jnp.abs(tokens_ref[...]).astype(jnp.float32), axis=0, keepdims=True)
    peaks = []
    for base in range(0, depth, BLOCK):
        top = jnp.abs(keyval_ref[base : base + BLOCK, :])
        for left in range(0, query_ref.shape[1], BLOCK):
            top = jnp.maximum(top, jnp.abs(query_ref[base : base + BLOCK, left : left + BLOCK]))
        peaks.append(across(top.astype(jnp.float32)))
    acts = [act[:, base : base + BLOCK] for base in range(0, depth, BLOCK)]
    both = jnp.concatenate(acts + peaks, axis=0).astype(jnp.bfloat16)
    peers = out_ref.shape[0] // 2
    for core in range(2):
        for block in range(depth // BLOCK):
            rows = tokens_ref[core * half : (core + 1) * half, block * BLOCK : (block + 1) * BLOCK]
            for peer in range(peers):
                out_ref[core * peers + peer, block * half : (block + 1) * half, :] = rows
        for peer in range(peers):
            out_ref[core * peers + peer, depth // BLOCK * half :, :] = both


def smooth_kernel(gathered_ref, smooth_ref, out_ref):
    members, packed, _ = gathered_ref.shape
    blocks = smooth_ref.shape[2] // BLOCK
    half = packed // blocks - 2
    peers = members // 2
    inverses = []
    for core in range(2):
        both = gathered_ref[core * peers, blocks * half :, :]
        for peer in range(1, peers):
            both = jnp.maximum(both, gathered_ref[core * peers + peer, blocks * half :, :])
        both = both.astype(jnp.float32)
        smooth = jnp.sqrt((both[:blocks] + EPSILON) / (both[blocks:] + EPSILON))
        inverse = 1.0 / smooth
        for block in range(blocks):
            lanes = slice(block * BLOCK, (block + 1) * BLOCK)
            smooth_ref[core, 0:1, lanes] = smooth[block : block + 1]
            smooth_ref[core, 1:2, lanes] = inverse[block : block + 1]
        inverses.append(inverse)
    per_block = BLOCK // half
    lines = []
    for first in range(0, peers, per_block):
        top = None
        for core in range(2):
            start = core * peers + first
            for block in range(blocks):
                rows = slice(block * half, (block + 1) * half)
                piece = jnp.abs(gathered_ref[start : start + per_block, rows, :])
                piece = piece.astype(jnp.float32).reshape(BLOCK, BLOCK)
                piece = piece * inverses[core][block : block + 1]
                top = piece if top is None else jnp.maximum(top, piece)
        lines.append(across(top))
    peak = jnp.concatenate(lines, axis=0)
    for copy in range(out_ref.shape[0]):
        out_ref[copy] = peak


def weights_kernel(
    core_ref, query_ref, keyval_ref, smooth_ref, send_ref, query_out, query_scale, keyval_out, keyval_scale
):
    smooth = smooth_ref[core_ref[0]][0:1, :]
    depth = query_ref.shape[0]
    lines = []
    for source, code_ref, scale_ref in (
        (query_ref, query_out, query_scale),
        (keyval_ref, keyval_out, keyval_scale),
    ):
        for row, base in enumerate(range(0, depth, BLOCK)):
            factor = down(smooth[:, base : base + BLOCK])
            scales = []
            for column, left in enumerate(range(0, source.shape[1], BLOCK)):
                block = source[base : base + BLOCK, left : left + BLOCK].astype(jnp.float32) * factor
                top = jnp.max(jnp.max(jnp.abs(block), axis=0, keepdims=True), axis=1, keepdims=True)
                scale = (top + EPSILON) / QSTEPS
                scale_ref[row : row + 1, column : column + 1] = scale
                scales.append(jnp.broadcast_to(scale, (1, BLOCK)))
                code = soften(block * (1.0 / scale)).astype(jnp.bfloat16)
                code_ref[base : base + BLOCK, left : left + BLOCK] = code
                if source is query_ref:
                    send_ref[base : base + BLOCK, left : left + BLOCK] = code
            if source is query_ref:
                lines.append(jnp.concatenate(scales, axis=1))
    rest = jnp.concatenate(lines, axis=0)
    pieces = []
    for _ in range(3):
        piece = rest.astype(jnp.bfloat16).astype(jnp.float32)
        rest = rest - piece
        pieces.append(piece)
    pieces.append(jnp.zeros_like(rest))
    send_ref[depth:, :] = jnp.concatenate(pieces, axis=0).astype(jnp.bfloat16)


def project_kernel(places, core_ref, gathered_ref, smooth_ref, peaks_ref, mine_ref, other_ref, out_ref):
    members, _, _ = gathered_ref.shape
    depth = smooth_ref.shape[2]
    half = out_ref.shape[1]
    peers = members // 2
    peak = peaks_ref[0]
    for member in range(1, peaks_ref.shape[0]):
        peak = jnp.maximum(peak, peaks_ref[member])
    scale = ((peak + EPSILON) / QSTEPS).astype(jnp.bfloat16).astype(jnp.float32)
    per_block = BLOCK // half
    blocks = depth // BLOCK
    sides = []
    for core, code_ref in ((core_ref[0], mine_ref), (1 - core_ref[0], other_ref)):
        pieces = code_ref[depth:, :].astype(jnp.float32)
        column_scale = pieces[0:blocks] + pieces[blocks : 2 * blocks] + pieces[2 * blocks : 3 * blocks]
        sides.append((core * peers, smooth_ref[core][1:2, :], code_ref, column_scale))
    for index, first in enumerate(range(0, peers, per_block)):
        row_scale = down(scale[index : index + 1, :])
        row_inverse = 1.0 / row_scale
        total = None
        for start, inverse, code_ref, column_scale in sides:
            for a in range(blocks):
                left = a * BLOCK
                piece = gathered_ref[pl.ds(start + first, per_block), a * half : (a + 1) * half, :]
                piece = piece.astype(jnp.float32).reshape(BLOCK, BLOCK)
                value = piece * inverse[:, left : left + BLOCK] * row_inverse
                code = soften(value).astype(jnp.bfloat16)
                product = jnp.dot(
                    code, code_ref[left : left + BLOCK, :], preferred_element_type=jnp.float32
                )
                product = product * column_scale[a : a + 1]
                total = product if total is None else total + product
        width = total.shape[1]
        total = jnp.concatenate(
            [total[:, c : c + BLOCK] * row_scale for c in range(0, width, BLOCK)], axis=1
        )
        total = total.astype(out_ref.dtype)
        for peer in range(per_block):
            out_ref[places[first + peer]] = total[peer * half : (peer + 1) * half]


def sum_kernel(parts_ref, out_ref):
    total = parts_ref[0].astype(jnp.float32)
    for part in range(1, parts_ref.shape[0]):
        total = total + parts_ref[part].astype(jnp.float32)
    out_ref[...] = total.astype(out_ref.dtype)


def call(kernel, out_shape, args, flops=0, specs=None, scratch=(), name=None):
    outs = out_shape if isinstance(out_shape, (tuple, list)) else (out_shape,)
    moved = sum(a.size * a.dtype.itemsize for a in (*args, *outs))
    return pl.pallas_call(
        kernel,
        out_shape=out_shape,
        in_specs=specs or [VMEM] * len(args),
        out_specs=jax.tree.map(lambda _: VMEM, out_shape),
        scratch_shapes=scratch,
        cost_estimate=pl.CostEstimate(flops=flops, bytes_accessed=moved, transcendentals=0),
        compiler_params=pltpu.CompilerParams(vmem_limit_bytes=8 << 20),
        name=name,
    )(*args)


def exchange(array, axes, order):
    return lax.all_to_all(array, axes, 0, 0, tiled=True, axis_index_groups=[order])


def body(chips, columns, orders, tokens, query_weight, keyval_weight):
    f32, bf16 = jnp.float32, jnp.bfloat16
    shape = jax.ShapeDtypeStruct
    rows, depth = tokens.shape
    half = rows // 2
    width = query_weight.shape[1]
    blocks = depth // BLOCK
    chip_order, column_order = orders
    core_column_order = column_order + [columns + column for column in column_order]
    places = [chip_order.index(column) for column in column_order]
    arguments = (tokens, query_weight, keyval_weight)
    send = call(
        peaks_kernel,
        shape((2 * columns, blocks * (half + 2), BLOCK), bf16),
        arguments,
        specs=[HBM] * 3,
        scratch=[pltpu.VMEM(a.shape, a.dtype) for a in arguments] + [pltpu.SemaphoreType.DMA((3,))],
        name="peaks",
    )
    gathered = exchange(send, ("core", "y", "x"), core_column_order)
    smooth, row_peaks = call(
        smooth_kernel,
        (shape((2, 8, depth), f32), shape((chips, columns * half // BLOCK, BLOCK), f32)),
        (gathered,),
        name="smooth",
    )
    peaks = exchange(row_peaks, "z", chip_order)
    core = lax.axis_index("core").astype(jnp.int32).reshape(1)
    mine, query_code, query_scale, keyval_code, keyval_scale = call(
        weights_kernel,
        (
            shape((depth + 4 * blocks, width), bf16),
            shape(query_weight.shape, bf16),
            shape((blocks, width // BLOCK), f32),
            shape(keyval_weight.shape, bf16),
            shape((blocks, keyval_weight.shape[1] // BLOCK), f32),
        ),
        (core, query_weight, keyval_weight, smooth),
        specs=[SMEM] + [VMEM] * 3,
        flops=20 * (query_weight.size + keyval_weight.size),
        name="weights",
    )
    other = lax.ppermute(mine, "core", [(0, 1), (1, 0)])
    partial = call(
        functools.partial(project_kernel, places),
        shape((chips, half, width), bf16),
        (core, gathered, smooth, peaks, mine, other),
        specs=[SMEM] + [VMEM] * 5,
        flops=2 * columns * rows * depth * width,
        name="project",
    )
    parts = exchange(partial, "z", chip_order)
    query_proj = call(sum_kernel, shape((half, width), bf16), (parts,), name="sum")
    return (query_proj, query_code, query_scale, keyval_code, keyval_scale)


def solution(mesh):
    rows, columns = mesh.devices.shape
    chips = rows // 2
    width = int(round(columns**0.5))
    height = columns // width
    fine = Mesh(mesh.devices.reshape(chips, 2, height, width), ("z", "core", "y", "x"))
    row, col = ("z", "core"), ("y", "x")
    far = lambda size: [(index + size // 2) % size for index in range(size)]
    orders = (far(chips), [y * width + x for y in far(height) for x in far(width)])
    return jax.shard_map(
        functools.partial(body, chips, columns, orders),
        mesh=fine,
        in_specs=(P(col, row), P(row, col), P(row, col)),
        out_specs=(P(row, col),) * 5,
        check_vma=False,
    )
```

```python
import functools

import jax
import jax.numpy as jnp
from jax import lax
from jax.experimental import pallas as pl
from jax.experimental.pallas import tpu as pltpu
from jax.sharding import Mesh, PartitionSpec as P


BLOCK = 128
QSTEPS = 4
EPSILON = 1e-06
ROUNDER = 12582912.0
SINE = (
    0.8999999761581421,
    -5.921761989593506,
    11.689058303833008,
    -10.986687660217285,
    6.018372535705566,
    -2.1297717094421387,
    0.45832234621047974,
)
VMEM = pl.BlockSpec(memory_space=pltpu.VMEM)
SMEM = pl.BlockSpec(memory_space=pltpu.SMEM)
HBM = pl.BlockSpec(memory_space=pltpu.HBM)


def soften(value):
    offset = value - ((value + ROUNDER) - ROUNDER)
    square = offset * offset
    series = SINE[-1]
    for term in SINE[-2::-1]:
        series = series * square + term
    return value - offset * series


def across(column_major):
    return jnp.max(column_major.T, axis=0, keepdims=True)


def down(row):
    return jnp.broadcast_to(row, (BLOCK, BLOCK)).T


def peaks_kernel(_, tokens_hbm, query_hbm, keyval_hbm, out_ref, tokens_ref, query_ref, keyval_ref, sems):
    copies = [
        pltpu.make_async_copy(source, target, sems.at[index])
        for index, (source, target) in enumerate(
            ((query_hbm, query_ref), (keyval_hbm, keyval_ref), (tokens_hbm, tokens_ref))
        )
    ]
    for copy in copies:
        copy.start()
    for copy in copies:
        copy.wait()
    depth = query_ref.shape[0]
    half = tokens_ref.shape[0] // 2
    act = jnp.max(jnp.abs(tokens_ref[...]).astype(jnp.float32), axis=0, keepdims=True)
    peaks = []
    for base in range(0, depth, BLOCK):
        top = jnp.abs(keyval_ref[base : base + BLOCK, :])
        for left in range(0, query_ref.shape[1], BLOCK):
            top = jnp.maximum(top, jnp.abs(query_ref[base : base + BLOCK, left : left + BLOCK]))
        peaks.append(across(top.astype(jnp.float32)))
    acts = [act[:, base : base + BLOCK] for base in range(0, depth, BLOCK)]
    both = jnp.concatenate(acts + peaks, axis=0).astype(jnp.bfloat16)
    peers = out_ref.shape[0] // 2
    for core in range(2):
        for block in range(depth // BLOCK):
            rows = tokens_ref[core * half : (core + 1) * half, block * BLOCK : (block + 1) * BLOCK]
            for peer in range(peers):
                out_ref[core * peers + peer, block * half : (block + 1) * half, :] = rows
        for peer in range(peers):
            out_ref[core * peers + peer, depth // BLOCK * half :, :] = both


def smooth_kernel(gathered_ref, smooth_ref, out_ref):
    members, packed, _ = gathered_ref.shape
    blocks = smooth_ref.shape[2] // BLOCK
    half = packed // blocks - 2
    peers = members // 2
    inverses = []
    for core in range(2):
        both = gathered_ref[core * peers, blocks * half :, :]
        for peer in range(1, peers):
            both = jnp.maximum(both, gathered_ref[core * peers + peer, blocks * half :, :])
        both = both.astype(jnp.float32)
        smooth = jnp.sqrt((both[:blocks] + EPSILON) / (both[blocks:] + EPSILON))
        inverse = 1.0 / smooth
        for block in range(blocks):
            lanes = slice(block * BLOCK, (block + 1) * BLOCK)
            smooth_ref[core, 0:1, lanes] = smooth[block : block + 1]
            smooth_ref[core, 1:2, lanes] = inverse[block : block + 1]
        inverses.append(inverse)
    per_block = BLOCK // half
    lines = []
    for first in range(0, peers, per_block):
        top = None
        for core in range(2):
            start = core * peers + first
            for block in range(blocks):
                rows = slice(block * half, (block + 1) * half)
                piece = jnp.abs(gathered_ref[start : start + per_block, rows, :])
                piece = piece.astype(jnp.float32).reshape(BLOCK, BLOCK)
                piece = piece * inverses[core][block : block + 1]
                top = piece if top is None else jnp.maximum(top, piece)
        lines.append(across(top))
    peak = jnp.concatenate(lines, axis=0)
    for copy in range(out_ref.shape[0]):
        out_ref[copy] = peak


def weights_kernel(
    core_ref, query_ref, keyval_ref, smooth_ref, send_ref, query_out, query_scale, keyval_out, keyval_scale
):
    smooth = smooth_ref[core_ref[0]][0:1, :]
    depth = query_ref.shape[0]
    lines = []
    for source, code_ref, scale_ref in (
        (query_ref, query_out, query_scale),
        (keyval_ref, keyval_out, keyval_scale),
    ):
        for row, base in enumerate(range(0, depth, BLOCK)):
            factor = down(smooth[:, base : base + BLOCK])
            scales = []
            for column, left in enumerate(range(0, source.shape[1], BLOCK)):
                block = source[base : base + BLOCK, left : left + BLOCK].astype(jnp.float32) * factor
                top = jnp.max(jnp.max(jnp.abs(block), axis=0, keepdims=True), axis=1, keepdims=True)
                scale = (top + EPSILON) / QSTEPS
                if source is query_ref:
                    scale_ref[row : row + 1, column : column + 1] = scale
                else:
                    scale_ref[column : column + 1, row : row + 1] = scale
                scales.append(jnp.broadcast_to(scale, (1, BLOCK)))
                code = soften(block * (1.0 / scale)).astype(jnp.bfloat16)
                code_ref[base : base + BLOCK, left : left + BLOCK] = code
                if source is query_ref:
                    send_ref[base : base + BLOCK, left : left + BLOCK] = code
            if source is query_ref:
                lines.append(jnp.concatenate(scales, axis=1))
    rest = jnp.concatenate(lines, axis=0)
    pieces = []
    for _ in range(3):
        piece = rest.astype(jnp.bfloat16).astype(jnp.float32)
        rest = rest - piece
        pieces.append(piece)
    pieces.append(jnp.zeros_like(rest))
    send_ref[depth:, :] = jnp.concatenate(pieces, axis=0).astype(jnp.bfloat16)


def project_kernel(places, core_ref, gathered_ref, smooth_ref, peaks_ref, mine_ref, other_ref, out_ref):
    members, _, _ = gathered_ref.shape
    depth = smooth_ref.shape[2]
    half = out_ref.shape[1]
    peers = members // 2
    peak = peaks_ref[0]
    for member in range(1, peaks_ref.shape[0]):
        peak = jnp.maximum(peak, peaks_ref[member])
    scale = ((peak + EPSILON) / QSTEPS).astype(jnp.bfloat16).astype(jnp.float32)
    per_block = BLOCK // half
    blocks = depth // BLOCK
    sides = []
    for core, code_ref in ((core_ref[0], mine_ref), (1 - core_ref[0], other_ref)):
        pieces = code_ref[depth:, :].astype(jnp.float32)
        column_scale = pieces[0:blocks] + pieces[blocks : 2 * blocks] + pieces[2 * blocks : 3 * blocks]
        sides.append((core * peers, smooth_ref[core][1:2, :], code_ref, column_scale))
    for index, first in enumerate(range(0, peers, per_block)):
        row_scale = down(scale[index : index + 1, :])
        row_inverse = 1.0 / row_scale
        total = None
        for start, inverse, code_ref, column_scale in sides:
            for a in range(blocks):
                left = a * BLOCK
                piece = gathered_ref[pl.ds(start + first, per_block), a * half : (a + 1) * half, :]
                piece = piece.astype(jnp.float32).reshape(BLOCK, BLOCK)
                value = piece * inverse[:, left : left + BLOCK] * row_inverse
                code = soften(value).astype(jnp.bfloat16)
                product = jnp.dot(
                    code, code_ref[left : left + BLOCK, :], preferred_element_type=jnp.float32
                )
                product = product * column_scale[a : a + 1]
                total = product if total is None else total + product
        width = total.shape[1]
        total = jnp.concatenate(
            [total[:, c : c + BLOCK] * row_scale for c in range(0, width, BLOCK)], axis=1
        )
        total = total.astype(out_ref.dtype)
        for peer in range(per_block):
            out_ref[places[first + peer]] = total[peer * half : (peer + 1) * half]


def sum_kernel(parts_ref, out_ref):
    total = parts_ref[0].astype(jnp.float32)
    for part in range(1, parts_ref.shape[0]):
        total = total + parts_ref[part].astype(jnp.float32)
    out_ref[...] = total.astype(out_ref.dtype)


def call(kernel, out_shape, args, **options):
    return launch(kernel, out_shape, args, **options)


def launch(kernel, out_shape, args, flops=0, specs=None, scratch=()):
    outs = out_shape if isinstance(out_shape, (tuple, list)) else (out_shape,)
    moved = sum(a.size * a.dtype.itemsize for a in (*args, *outs))
    return pl.pallas_call(
        kernel,
        out_shape=out_shape,
        in_specs=specs or [VMEM] * len(args),
        out_specs=jax.tree.map(lambda _: VMEM, out_shape),
        scratch_shapes=scratch,
        cost_estimate=pl.CostEstimate(flops=flops, bytes_accessed=moved, transcendentals=0),
        compiler_params=pltpu.CompilerParams(vmem_limit_bytes=8 << 20),
    )(*args)


def exchange(array, axes, order):
    return lax.all_to_all(array, axes, 0, 0, tiled=True, axis_index_groups=[order])


def body(chips, columns, orders, tokens, query_weight, keyval_weight):
    f32, bf16 = jnp.float32, jnp.bfloat16
    shape = jax.ShapeDtypeStruct
    rows, depth = tokens.shape
    half = rows // 2
    width = query_weight.shape[1]
    blocks = depth // BLOCK
    chip_order, column_order = orders
    core_column_order = column_order + [columns + column for column in column_order]
    places = [chip_order.index(column) for column in column_order]
    arguments = (tokens, query_weight, keyval_weight)
    core = lax.axis_index("core").astype(jnp.int32).reshape(1)
    send = call(
        peaks_kernel,
        shape((2 * columns, blocks * (half + 2), BLOCK), bf16),
        (core, *(pltpu.with_memory_space_constraint(a, pltpu.HBM) for a in arguments)),
        specs=[SMEM] + [HBM] * 3,
        scratch=[pltpu.VMEM(a.shape, a.dtype) for a in arguments] + [pltpu.SemaphoreType.DMA((3,))],
    )
    gathered = exchange(send, ("core", "y", "x"), core_column_order)
    smooth, row_peaks = call(
        smooth_kernel,
        (shape((2, 8, depth), f32), shape((chips, columns * half // BLOCK, BLOCK), f32)),
        (gathered,),
    )
    peaks = exchange(row_peaks, "z", chip_order)
    mine, query_code, query_scale, keyval_code, keyval_scale = call(
        weights_kernel,
        (
            shape((depth + 4 * blocks, width), bf16),
            shape(query_weight.shape, bf16),
            shape((blocks, width // BLOCK), f32),
            shape(keyval_weight.shape, bf16),
            shape((keyval_weight.shape[1] // BLOCK, blocks), f32),
        ),
        (core, query_weight, keyval_weight, smooth),
        specs=[SMEM] + [VMEM] * 3,
        flops=20 * (query_weight.size + keyval_weight.size),
    )
    other = lax.ppermute(mine, "core", [(0, 1), (1, 0)])
    partial = call(
        functools.partial(project_kernel, places),
        shape((chips, half, width), bf16),
        (core, gathered, smooth, peaks, mine, other),
        specs=[SMEM] + [VMEM] * 5,
        flops=2 * columns * rows * depth * width,
    )
    parts = exchange(partial, "z", chip_order)
    query_proj = call(sum_kernel, shape((half, width), bf16), (parts,))
    return (query_proj, query_code, query_scale, keyval_code, keyval_scale.T)


def solution(mesh):
    rows, columns = mesh.devices.shape
    chips = rows // 2
    width = int(round(columns**0.5))
    height = columns // width
    fine = Mesh(mesh.devices.reshape(chips, 2, height, width), ("z", "core", "y", "x"))
    row, col = ("z", "core"), ("y", "x")
    far = lambda size: [(index + size // 2) % size for index in range(size)]
    orders = (far(chips), [y * width + x for y in far(height) for x in far(width)])
    return jax.shard_map(
        functools.partial(body, chips, columns, orders),
        mesh=fine,
        in_specs=(P(col, row), P(row, col), P(row, col)),
        out_specs=(P(row, col),) * 5,
        check_vma=False,
    )
```

```python
import functools

import jax
import jax.numpy as jnp
from jax import lax
from jax.experimental import pallas as pl
from jax.experimental.pallas import tpu as pltpu
from jax.sharding import Mesh, PartitionSpec as P


BLOCK = 128
QSTEPS = 4
EPSILON = 1e-06
ROUNDER = 12582912.0
SINE = (
    0.8999999761581421,
    -5.921761989593506,
    11.689058303833008,
    -10.986687660217285,
    6.018372535705566,
    -2.1297717094421387,
    0.45832234621047974,
)
VMEM = pl.BlockSpec(memory_space=pltpu.VMEM)
SMEM = pl.BlockSpec(memory_space=pltpu.SMEM)
HBM = pl.BlockSpec(memory_space=pltpu.HBM)


def soften(value):
    offset = value - ((value + ROUNDER) - ROUNDER)
    square = offset * offset
    series = SINE[-1]
    for term in SINE[-2::-1]:
        series = series * square + term
    return value - offset * series


def across(column_major):
    return jnp.max(column_major.T, axis=0, keepdims=True)


def down(row):
    return jnp.broadcast_to(row, (BLOCK, BLOCK)).T


def peaks_kernel(_, tokens_hbm, query_hbm, keyval_hbm, out_ref, tokens_ref, query_ref, keyval_ref, sems):
    copies = [
        pltpu.make_async_copy(source, target, sems.at[index])
        for index, (source, target) in enumerate(
            ((query_hbm, query_ref), (keyval_hbm, keyval_ref), (tokens_hbm, tokens_ref))
        )
    ]
    for copy in copies:
        copy.start()
    for copy in copies:
        copy.wait()
    depth = query_ref.shape[0]
    half = tokens_ref.shape[0] // 2
    act = jnp.max(jnp.abs(tokens_ref[...]).astype(jnp.float32), axis=0, keepdims=True)
    peaks = []
    for base in range(0, depth, BLOCK):
        top = jnp.abs(keyval_ref[base : base + BLOCK, :])
        for left in range(0, query_ref.shape[1], BLOCK):
            top = jnp.maximum(top, jnp.abs(query_ref[base : base + BLOCK, left : left + BLOCK]))
        peaks.append(across(top.astype(jnp.float32)))
    acts = [act[:, base : base + BLOCK] for base in range(0, depth, BLOCK)]
    both = jnp.concatenate(acts + peaks, axis=0).astype(jnp.bfloat16)
    peers = out_ref.shape[0] // 2
    for core in range(2):
        for block in range(depth // BLOCK):
            rows = tokens_ref[core * half : (core + 1) * half, block * BLOCK : (block + 1) * BLOCK]
            for peer in range(peers):
                out_ref[core * peers + peer, block * half : (block + 1) * half, :] = rows
        for peer in range(peers):
            out_ref[core * peers + peer, depth // BLOCK * half :, :] = both


def smooth_kernel(gathered_ref, smooth_ref, out_ref):
    members, packed, _ = gathered_ref.shape
    blocks = smooth_ref.shape[2] // BLOCK
    half = packed // blocks - 2
    peers = members // 2
    inverses = []
    for core in range(2):
        both = gathered_ref[core * peers, blocks * half :, :]
        for peer in range(1, peers):
            both = jnp.maximum(both, gathered_ref[core * peers + peer, blocks * half :, :])
        both = both.astype(jnp.float32)
        smooth = jnp.sqrt((both[:blocks] + EPSILON) / (both[blocks:] + EPSILON))
        inverse = 1.0 / smooth
        for block in range(blocks):
            lanes = slice(block * BLOCK, (block + 1) * BLOCK)
            smooth_ref[core, 0:1, lanes] = smooth[block : block + 1]
            smooth_ref[core, 1:2, lanes] = inverse[block : block + 1]
        inverses.append(inverse)
    per_block = BLOCK // half
    lines = []
    for first in range(0, peers, per_block):
        top = None
        for core in range(2):
            start = core * peers + first
            for block in range(blocks):
                rows = slice(block * half, (block + 1) * half)
                piece = jnp.abs(gathered_ref[start : start + per_block, rows, :])
                piece = piece.astype(jnp.float32).reshape(BLOCK, BLOCK)
                piece = piece * inverses[core][block : block + 1]
                top = piece if top is None else jnp.maximum(top, piece)
        lines.append(across(top))
    peak = jnp.concatenate(lines, axis=0)
    for copy in range(out_ref.shape[0]):
        out_ref[copy] = peak


def encode(core, query_ref, other_ref, keyval_ref, smooth_ref, outs):
    query_out, query_scale, mine_out, mine_scale, other_out, other_scale, keyval_out, keyval_scale = outs
    for source, side, targets in (
        (query_ref, core, ((query_out, query_scale), (mine_out, mine_scale))),
        (other_ref, 1 - core, ((other_out, other_scale),)),
        (keyval_ref, core, ((keyval_out, keyval_scale),)),
    ):
        smooth = smooth_ref[side][0:1, :]
        for row, base in enumerate(range(0, source.shape[0], BLOCK)):
            factor = down(smooth[:, base : base + BLOCK])
            for column, left in enumerate(range(0, source.shape[1], BLOCK)):
                block = source[base : base + BLOCK, left : left + BLOCK].astype(jnp.float32) * factor
                top = jnp.max(jnp.max(jnp.abs(block), axis=0, keepdims=True), axis=1, keepdims=True)
                scale = (top + EPSILON) / QSTEPS
                code = soften(block * (1.0 / scale)).astype(jnp.bfloat16)
                for code_ref, scale_ref in targets:
                    if source is keyval_ref:
                        scale_ref[column : column + 1, row : row + 1] = scale
                    else:
                        scale_ref[row : row + 1, column : column + 1] = scale
                    code_ref[base : base + BLOCK, left : left + BLOCK] = code


def weights_kernel(core_ref, query_ref, other_ref, keyval_ref, smooth_ref, *outs):
    encode(core_ref[0], query_ref, other_ref, keyval_ref, smooth_ref, outs)


def project_kernel(places, core_ref, gathered_ref, smooth_ref, peaks_ref, *refs):
    mine_ref, mine_scale, other_ref, other_scale, out_ref = refs
    members, _, _ = gathered_ref.shape
    depth = smooth_ref.shape[2]
    half = out_ref.shape[1]
    peers = members // 2
    peak = peaks_ref[0]
    for member in range(1, peaks_ref.shape[0]):
        peak = jnp.maximum(peak, peaks_ref[member])
    scale = ((peak + EPSILON) / QSTEPS).astype(jnp.bfloat16).astype(jnp.float32)
    per_block = BLOCK // half
    blocks = depth // BLOCK
    sides = []
    for core, code_ref, scale_ref in (
        (core_ref[0], mine_ref, mine_scale),
        (1 - core_ref[0], other_ref, other_scale),
    ):
        column_scale = [
            jnp.concatenate(
                [
                    jnp.broadcast_to(scale_ref[a : a + 1, c : c + 1], (1, BLOCK))
                    for c in range(scale_ref.shape[1])
                ],
                axis=1,
            )
            for a in range(blocks)
        ]
        sides.append((core * peers, smooth_ref[core][1:2, :], code_ref, column_scale))
    for index, first in enumerate(range(0, peers, per_block)):
        row_scale = down(scale[index : index + 1, :])
        row_inverse = 1.0 / row_scale
        total = None
        for start, inverse, code_ref, column_scale in sides:
            for a in range(blocks):
                left = a * BLOCK
                piece = gathered_ref[pl.ds(start + first, per_block), a * half : (a + 1) * half, :]
                piece = piece.astype(jnp.float32).reshape(BLOCK, BLOCK)
                value = piece * inverse[:, left : left + BLOCK] * row_inverse
                code = soften(value).astype(jnp.bfloat16)
                product = jnp.dot(
                    code, code_ref[left : left + BLOCK, :], preferred_element_type=jnp.float32
                )
                product = product * column_scale[a]
                total = product if total is None else total + product
        width = total.shape[1]
        total = jnp.concatenate(
            [total[:, c : c + BLOCK] * row_scale for c in range(0, width, BLOCK)], axis=1
        )
        total = total.astype(out_ref.dtype)
        for peer in range(per_block):
            out_ref[places[first + peer]] = total[peer * half : (peer + 1) * half]


def sum_kernel(parts_ref, out_ref):
    total = parts_ref[0].astype(jnp.float32)
    for part in range(1, parts_ref.shape[0]):
        total = total + parts_ref[part].astype(jnp.float32)
    out_ref[...] = total.astype(out_ref.dtype)


def call(kernel, out_shape, args, **options):
    return launch(kernel, out_shape, args, **options)


def launch(kernel, out_shape, args, flops=0, specs=None, scratch=()):
    outs = out_shape if isinstance(out_shape, (tuple, list)) else (out_shape,)
    moved = sum(a.size * a.dtype.itemsize for a in (*args, *outs))
    return pl.pallas_call(
        kernel,
        out_shape=out_shape,
        in_specs=specs or [VMEM] * len(args),
        out_specs=jax.tree.map(lambda _: VMEM, out_shape),
        scratch_shapes=scratch,
        cost_estimate=pl.CostEstimate(flops=flops, bytes_accessed=moved, transcendentals=0),
        compiler_params=pltpu.CompilerParams(vmem_limit_bytes=8 << 20),
    )(*args)


def exchange(array, axes, order):
    return lax.all_to_all(array, axes, 0, 0, tiled=True, axis_index_groups=[order])


def body(chips, columns, orders, tokens, query_weight, keyval_weight):
    f32, bf16 = jnp.float32, jnp.bfloat16
    shape = jax.ShapeDtypeStruct
    rows, depth = tokens.shape
    half = rows // 2
    width = query_weight.shape[1]
    blocks = depth // BLOCK
    peak_order, part_order, column_order = orders
    core_column_order = column_order + [columns + column for column in column_order]
    places = [part_order.index(column) for column in column_order]
    arguments = (tokens, query_weight, keyval_weight)
    core = lax.axis_index("core").astype(jnp.int32).reshape(1)
    send = call(
        peaks_kernel,
        shape((2 * columns, blocks * (half + 2), BLOCK), bf16),
        (core, *(pltpu.with_memory_space_constraint(a, pltpu.HBM) for a in arguments)),
        specs=[SMEM] + [HBM] * 3,
        scratch=[pltpu.VMEM(a.shape, a.dtype) for a in arguments] + [pltpu.SemaphoreType.DMA((3,))],
    )
    gathered = exchange(send, ("core", "y", "x"), core_column_order)
    other_weight = lax.ppermute(query_weight, "core", [(0, 1), (1, 0)])
    smooth, row_peaks = call(
        smooth_kernel,
        (shape((2, 8, depth), f32), shape((chips, columns * half // BLOCK, BLOCK), f32)),
        (gathered,),
    )
    peaks = exchange(row_peaks, "z", peak_order)
    code = shape(query_weight.shape, bf16)
    scale = shape((blocks, width // BLOCK), f32)
    query_code, query_scale, *both, keyval_code, keyval_scale = call(
        weights_kernel,
        (
            *(code, scale) * 3,
            shape(keyval_weight.shape, bf16),
            shape((keyval_weight.shape[1] // BLOCK, blocks), f32),
        ),
        (core, query_weight, other_weight, keyval_weight, smooth),
        specs=[SMEM] + [VMEM] * 4,
        flops=20 * (2 * query_weight.size + keyval_weight.size),
    )
    partial = call(
        functools.partial(project_kernel, places),
        shape((chips, half, width), bf16),
        (core, gathered, smooth, peaks, *both),
        specs=[SMEM] + [VMEM] * 7,
        flops=2 * columns * rows * depth * width,
    )
    parts = exchange(partial, "z", part_order)
    query_proj = call(sum_kernel, shape((half, width), bf16), (parts,))
    return (query_proj, query_code, query_scale, keyval_code, keyval_scale.T)


def solution(mesh):
    rows, columns = mesh.devices.shape
    chips = rows // 2
    width = int(round(columns**0.5))
    height = columns // width
    fine = Mesh(mesh.devices.reshape(chips, 2, height, width), ("z", "core", "y", "x"))
    row, col = ("z", "core"), ("y", "x")
    turned = lambda size, first: [(index + first) % size for index in range(size)]
    orders = (
        turned(chips, 11 * chips // 16),
        turned(chips, chips // 2),
        [y * width + x for y in turned(height, height - 1) for x in turned(width, width - 1)],
    )
    return jax.shard_map(
        functools.partial(body, chips, columns, orders),
        mesh=fine,
        in_specs=(P(col, row), P(row, col), P(row, col)),
        out_specs=(P(row, col),) * 5,
        check_vma=False,
    )
```

```python
import functools

import jax
import jax.numpy as jnp
from jax import lax
from jax.experimental import pallas as pl
from jax.experimental.pallas import tpu as pltpu
from jax.sharding import Mesh, PartitionSpec as P


BLOCK = 128
QSTEPS = 4
EPSILON = 1e-06
ROUNDER = 12582912.0
SINE = (
    0.8999999761581421,
    -5.921761989593506,
    11.689058303833008,
    -10.986687660217285,
    6.018372535705566,
    -2.1297717094421387,
    0.45832234621047974,
)
VMEM = pl.BlockSpec(memory_space=pltpu.VMEM)
SMEM = pl.BlockSpec(memory_space=pltpu.SMEM)
HBM = pl.BlockSpec(memory_space=pltpu.HBM)


def soften(value):
    offset = value - ((value + ROUNDER) - ROUNDER)
    square = offset * offset
    series = SINE[-1]
    for term in SINE[-2::-1]:
        series = series * square + term
    return value - offset * series


def across(column_major):
    return jnp.max(column_major.T, axis=0, keepdims=True)


def down(row):
    return jnp.broadcast_to(row, (BLOCK, BLOCK)).T


def peaks_kernel(_, tokens_hbm, query_hbm, keyval_hbm, out_ref, tokens_ref, query_ref, keyval_ref, sems):
    copies = [
        pltpu.make_async_copy(source, target, sems.at[index])
        for index, (source, target) in enumerate(
            ((query_hbm, query_ref), (keyval_hbm, keyval_ref), (tokens_hbm, tokens_ref))
        )
    ]
    for copy in copies:
        copy.start()
    for copy in copies:
        copy.wait()
    depth = query_ref.shape[0]
    half = tokens_ref.shape[0] // 2
    act = jnp.max(jnp.abs(tokens_ref[...]).astype(jnp.float32), axis=0, keepdims=True)
    peaks = []
    for base in range(0, depth, BLOCK):
        top = jnp.abs(keyval_ref[base : base + BLOCK, :])
        for left in range(0, query_ref.shape[1], BLOCK):
            top = jnp.maximum(top, jnp.abs(query_ref[base : base + BLOCK, left : left + BLOCK]))
        peaks.append(across(top.astype(jnp.float32)))
    acts = [act[:, base : base + BLOCK] for base in range(0, depth, BLOCK)]
    both = jnp.concatenate(acts + peaks, axis=0).astype(jnp.bfloat16)
    peers = out_ref.shape[0] // 2
    for core in range(2):
        for block in range(depth // BLOCK):
            rows = tokens_ref[core * half : (core + 1) * half, block * BLOCK : (block + 1) * BLOCK]
            for peer in range(peers):
                out_ref[core * peers + peer, block * half : (block + 1) * half, :] = rows
        for peer in range(peers):
            out_ref[core * peers + peer, depth // BLOCK * half :, :] = both


def smooth_kernel(gathered_ref, smooth_ref, out_ref):
    members, packed, _ = gathered_ref.shape
    blocks = smooth_ref.shape[2] // BLOCK
    half = packed // blocks - 2
    peers = members // 2
    inverses = []
    for core in range(2):
        both = gathered_ref[core * peers, blocks * half :, :]
        for peer in range(1, peers):
            both = jnp.maximum(both, gathered_ref[core * peers + peer, blocks * half :, :])
        both = both.astype(jnp.float32)
        smooth = jnp.sqrt((both[:blocks] + EPSILON) / (both[blocks:] + EPSILON))
        inverse = 1.0 / smooth
        for block in range(blocks):
            lanes = slice(block * BLOCK, (block + 1) * BLOCK)
            smooth_ref[core, 0:1, lanes] = smooth[block : block + 1]
            smooth_ref[core, 1:2, lanes] = inverse[block : block + 1]
        inverses.append(inverse)
    per_block = BLOCK // half
    lines = []
    for first in range(0, peers, per_block):
        top = None
        for core in range(2):
            start = core * peers + first
            for block in range(blocks):
                rows = slice(block * half, (block + 1) * half)
                piece = jnp.abs(gathered_ref[start : start + per_block, rows, :])
                piece = piece.astype(jnp.float32).reshape(BLOCK, BLOCK)
                piece = piece * inverses[core][block : block + 1]
                top = piece if top is None else jnp.maximum(top, piece)
        lines.append(across(top))
    peak = jnp.concatenate(lines, axis=0)
    for copy in range(out_ref.shape[0]):
        out_ref[copy] = peak


def encode(core, query_ref, other_ref, keyval_ref, smooth_ref, outs):
    query_out, query_scale, mine_out, mine_scale, other_out, other_scale, keyval_out, keyval_scale = outs
    for source, side, targets in (
        (query_ref, core, ((query_out, query_scale), (mine_out, mine_scale))),
        (other_ref, 1 - core, ((other_out, other_scale),)),
        (keyval_ref, core, ((keyval_out, keyval_scale),)),
    ):
        smooth = smooth_ref[side][0:1, :]
        for row, base in enumerate(range(0, source.shape[0], BLOCK)):
            factor = down(smooth[:, base : base + BLOCK])
            for column, left in enumerate(range(0, source.shape[1], BLOCK)):
                block = source[base : base + BLOCK, left : left + BLOCK].astype(jnp.float32) * factor
                top = jnp.max(jnp.max(jnp.abs(block), axis=0, keepdims=True), axis=1, keepdims=True)
                scale = (top + EPSILON) / QSTEPS
                code = soften(block * (1.0 / scale)).astype(jnp.bfloat16)
                for code_ref, scale_ref in targets:
                    if source is keyval_ref:
                        scale_ref[column : column + 1, row : row + 1] = scale
                    else:
                        scale_ref[row : row + 1, column : column + 1] = scale
                    code_ref[base : base + BLOCK, left : left + BLOCK] = code


def weights_kernel(core_ref, query_ref, other_ref, keyval_ref, smooth_ref, *outs):
    encode(core_ref[0], query_ref, other_ref, keyval_ref, smooth_ref, outs)


def project_kernel(places, core_ref, gathered_ref, smooth_ref, peaks_ref, *refs):
    mine_ref, mine_scale, other_ref, other_scale, out_ref = refs
    members, _, _ = gathered_ref.shape
    depth = smooth_ref.shape[2]
    half = out_ref.shape[1]
    peers = members // 2
    peak = peaks_ref[0]
    for member in range(1, peaks_ref.shape[0]):
        peak = jnp.maximum(peak, peaks_ref[member])
    scale = ((peak + EPSILON) / QSTEPS).astype(jnp.bfloat16).astype(jnp.float32)
    per_block = BLOCK // half
    blocks = depth // BLOCK
    sides = []
    for core, code_ref, scale_ref in (
        (core_ref[0], mine_ref, mine_scale),
        (1 - core_ref[0], other_ref, other_scale),
    ):
        column_scale = [
            jnp.concatenate(
                [
                    jnp.broadcast_to(scale_ref[a : a + 1, c : c + 1], (1, BLOCK))
                    for c in range(scale_ref.shape[1])
                ],
                axis=1,
            )
            for a in range(blocks)
        ]
        sides.append((core * peers, smooth_ref[core][1:2, :], code_ref, column_scale))
    for index, first in enumerate(range(0, peers, per_block)):
        row_scale = down(scale[index : index + 1, :])
        row_inverse = 1.0 / row_scale
        total = None
        for start, inverse, code_ref, column_scale in sides:
            for a in range(blocks):
                left = a * BLOCK
                piece = gathered_ref[pl.ds(start + first, per_block), a * half : (a + 1) * half, :]
                piece = piece.astype(jnp.float32).reshape(BLOCK, BLOCK)
                value = piece * inverse[:, left : left + BLOCK] * row_inverse
                code = soften(value).astype(jnp.bfloat16)
                product = jnp.dot(
                    code, code_ref[left : left + BLOCK, :], preferred_element_type=jnp.float32
                )
                product = product * column_scale[a]
                total = product if total is None else total + product
        width = total.shape[1]
        total = jnp.concatenate(
            [total[:, c : c + BLOCK] * row_scale for c in range(0, width, BLOCK)], axis=1
        )
        total = total.astype(out_ref.dtype)
        for peer in range(per_block):
            out_ref[places[first + peer]] = total[peer * half : (peer + 1) * half]


def sum_kernel(parts_ref, out_ref):
    total = parts_ref[0].astype(jnp.float32)
    for part in range(1, parts_ref.shape[0]):
        total = total + parts_ref[part].astype(jnp.float32)
    out_ref[...] = total.astype(out_ref.dtype)


def call(kernel, out_shape, args, **options):
    return launch(kernel, out_shape, args, **options)


def launch(kernel, out_shape, args, flops=0, specs=None, scratch=()):
    outs = out_shape if isinstance(out_shape, (tuple, list)) else (out_shape,)
    moved = sum(a.size * a.dtype.itemsize for a in (*args, *outs))
    return pl.pallas_call(
        kernel,
        out_shape=out_shape,
        in_specs=specs or [VMEM] * len(args),
        out_specs=jax.tree.map(lambda _: VMEM, out_shape),
        scratch_shapes=scratch,
        cost_estimate=pl.CostEstimate(flops=flops, bytes_accessed=moved, transcendentals=0),
        compiler_params=pltpu.CompilerParams(vmem_limit_bytes=8 << 20),
    )(*args)


def exchange(array, axes, order):
    return lax.all_to_all(array, axes, 0, 0, tiled=True, axis_index_groups=[order])


def body(chips, columns, orders, tokens, query_weight, keyval_weight):
    f32, bf16 = jnp.float32, jnp.bfloat16
    shape = jax.ShapeDtypeStruct
    rows, depth = tokens.shape
    half = rows // 2
    width = query_weight.shape[1]
    blocks = depth // BLOCK
    peak_order, part_order, column_order = orders
    core_column_order = column_order + [columns + column for column in column_order]
    places = [part_order.index(column) for column in column_order]
    arguments = (tokens, query_weight, keyval_weight)
    core = lax.axis_index("core").astype(jnp.int32).reshape(1)
    send = call(
        peaks_kernel,
        shape((2 * columns, blocks * (half + 2), BLOCK), bf16),
        (core, *(pltpu.with_memory_space_constraint(a, pltpu.HBM) for a in arguments)),
        specs=[SMEM] + [HBM] * 3,
        scratch=[pltpu.VMEM(a.shape, a.dtype) for a in arguments] + [pltpu.SemaphoreType.DMA((3,))],
    )
    gathered = exchange(send, ("core", "y", "x"), core_column_order)
    other_weight = lax.ppermute(query_weight, "core", [(0, 1), (1, 0)])
    smooth, row_peaks = call(
        smooth_kernel,
        (shape((2, 8, depth), f32), shape((chips, columns * half // BLOCK, BLOCK), f32)),
        (gathered,),
    )
    peaks = exchange(row_peaks, "z", peak_order)
    code = shape(query_weight.shape, bf16)
    scale = shape((blocks, width // BLOCK), f32)
    query_code, query_scale, *both, keyval_code, keyval_scale = call(
        weights_kernel,
        (
            *(code, scale) * 3,
            shape(keyval_weight.shape, bf16),
            shape((keyval_weight.shape[1] // BLOCK, blocks), f32),
        ),
        (core, query_weight, other_weight, keyval_weight, smooth),
        specs=[SMEM] + [VMEM] * 4,
        flops=20 * (2 * query_weight.size + keyval_weight.size),
    )
    partial = call(
        functools.partial(project_kernel, places),
        shape((chips, half, width), bf16),
        (core, gathered, smooth, peaks, *both),
        specs=[SMEM] + [VMEM] * 7,
        flops=2 * columns * rows * depth * width,
    )
    parts = exchange(partial, "z", part_order)
    query_proj = call(sum_kernel, shape((half, width), bf16), (parts,))
    return (query_proj, query_code, query_scale, keyval_code, keyval_scale.T)


def solution(mesh):
    rows, columns = mesh.devices.shape
    chips = rows // 2
    width = int(round(columns**0.5))
    height = columns // width
    fine = Mesh(mesh.devices.reshape(chips, 2, height, width), ("z", "core", "y", "x"))
    row, col = ("z", "core"), ("y", "x")
    turned = lambda size, first: [(index + first) % size for index in range(size)]
    facing = lambda size, first: [
        (first + index + side * size // 2) % size for index in range(size // 2) for side in range(2)
    ]
    orders = (
        facing(chips, 11 * chips // 16),
        facing(chips, chips // 2),
        [y * width + x for y in turned(height, height - 1) for x in turned(width, width - 1)],
    )
    return jax.shard_map(
        functools.partial(body, chips, columns, orders),
        mesh=fine,
        in_specs=(P(col, row), P(row, col), P(row, col)),
        out_specs=(P(row, col),) * 5,
        check_vma=False,
    )
```

```python
import functools

import jax
import jax.numpy as jnp
from jax import lax
from jax.experimental import pallas as pl
from jax.experimental.pallas import tpu as pltpu
from jax.sharding import Mesh, PartitionSpec as P


BLOCK = 128
QSTEPS = 4
EPSILON = 1e-06
ROUNDER = 12582912.0
SINE = (
    0.8999999761581421,
    -5.921761989593506,
    11.689058303833008,
    -10.986687660217285,
    6.018372535705566,
    -2.1297717094421387,
    0.45832234621047974,
)
VMEM = pl.BlockSpec(memory_space=pltpu.VMEM)
SMEM = pl.BlockSpec(memory_space=pltpu.SMEM)
HBM = pl.BlockSpec(memory_space=pltpu.HBM)


def soften(value):
    offset = value - ((value + ROUNDER) - ROUNDER)
    square = offset * offset
    series = SINE[-1]
    for term in SINE[-2::-1]:
        series = series * square + term
    return value - offset * series


def across(column_major):
    return jnp.max(column_major.T, axis=0, keepdims=True)


def down(row):
    return jnp.broadcast_to(row, (BLOCK, BLOCK)).T


def peaks_kernel(_, tokens_hbm, query_hbm, keyval_hbm, out_hbm, *scratch):
    tokens_ref, query_ref, keyval_ref, rows_ref, both_ref, load_sems, send_sems = scratch
    loads = [
        pltpu.make_async_copy(source, target, load_sems.at[index])
        for index, (source, target) in enumerate(
            ((tokens_hbm, tokens_ref), (query_hbm, query_ref), (keyval_hbm, keyval_ref))
        )
    ]
    for load in loads:
        load.start()
    depth = query_ref.shape[0]
    half = tokens_ref.shape[0] // 2
    body = depth // BLOCK * half
    members = out_hbm.shape[0]
    loads[0].wait()
    for core in range(2):
        for block in range(depth // BLOCK):
            rows = tokens_ref[core * half : (core + 1) * half, block * BLOCK : (block + 1) * BLOCK]
            for peer in range(members // 2):
                rows_ref[(1 - core) * members // 2 + peer, block * half : (block + 1) * half, :] = rows
    sends = [
        pltpu.make_async_copy(rows_ref, out_hbm.at[:, pl.ds(0, body), :], send_sems.at[0]),
        pltpu.make_async_copy(both_ref, out_hbm.at[:, pl.ds(body, both_ref.shape[1]), :], send_sems.at[1]),
    ]
    sends[0].start()
    act = jnp.max(jnp.abs(tokens_ref[...]).astype(jnp.float32), axis=0, keepdims=True)
    acts = [act[:, base : base + BLOCK] for base in range(0, depth, BLOCK)]
    loads[1].wait()
    loads[2].wait()
    peaks = []
    for base in range(0, depth, BLOCK):
        top = jnp.abs(keyval_ref[base : base + BLOCK, :])
        for left in range(0, query_ref.shape[1], BLOCK):
            top = jnp.maximum(top, jnp.abs(query_ref[base : base + BLOCK, left : left + BLOCK]))
        peaks.append(across(top.astype(jnp.float32)))
    both = jnp.concatenate(acts + peaks, axis=0).astype(jnp.bfloat16)
    for member in range(members):
        both_ref[member] = both
    sends[1].start()
    for send in sends:
        send.wait()


def smooth_kernel(gathered_ref, smooth_ref, out_ref):
    members, packed, _ = gathered_ref.shape
    blocks = smooth_ref.shape[2] // BLOCK
    half = packed // blocks - 2
    peers = members // 2
    inverses = []
    for core in range(2):
        both = gathered_ref[(1 - core) * peers, blocks * half :, :]
        for peer in range(1, peers):
            both = jnp.maximum(both, gathered_ref[(1 - core) * peers + peer, blocks * half :, :])
        both = both.astype(jnp.float32)
        smooth = jnp.sqrt((both[:blocks] + EPSILON) / (both[blocks:] + EPSILON))
        inverse = 1.0 / smooth
        for block in range(blocks):
            lanes = slice(block * BLOCK, (block + 1) * BLOCK)
            smooth_ref[core, 0:1, lanes] = smooth[block : block + 1]
            smooth_ref[core, 1:2, lanes] = inverse[block : block + 1]
        inverses.append(inverse)
    per_block = BLOCK // half
    lines = []
    for first in range(0, peers, per_block):
        top = None
        for core in range(2):
            start = (1 - core) * peers + first
            for block in range(blocks):
                rows = slice(block * half, (block + 1) * half)
                piece = jnp.abs(gathered_ref[start : start + per_block, rows, :])
                piece = piece.astype(jnp.float32).reshape(BLOCK, BLOCK)
                piece = piece * inverses[core][block : block + 1]
                top = piece if top is None else jnp.maximum(top, piece)
        lines.append(across(top))
    peak = jnp.concatenate(lines, axis=0)
    for copy in range(out_ref.shape[0]):
        out_ref[copy] = peak


def encode(core, query_ref, other_ref, keyval_ref, smooth_ref, outs):
    query_out, query_scale, mine_out, mine_scale, other_out, other_scale, keyval_out, keyval_scale = outs
    for source, side, targets in (
        (query_ref, core, ((query_out, query_scale), (mine_out, mine_scale))),
        (other_ref, 1 - core, ((other_out, other_scale),)),
        (keyval_ref, core, ((keyval_out, keyval_scale),)),
    ):
        smooth = smooth_ref[side][0:1, :]
        for row, base in enumerate(range(0, source.shape[0], BLOCK)):
            factor = down(smooth[:, base : base + BLOCK])
            for column, left in enumerate(range(0, source.shape[1], BLOCK)):
                block = source[base : base + BLOCK, left : left + BLOCK].astype(jnp.float32) * factor
                top = jnp.max(jnp.max(jnp.abs(block), axis=0, keepdims=True), axis=1, keepdims=True)
                scale = (top + EPSILON) / QSTEPS
                code = soften(block * (1.0 / scale)).astype(jnp.bfloat16)
                for code_ref, scale_ref in targets:
                    if source is keyval_ref:
                        scale_ref[column : column + 1, row : row + 1] = scale
                    else:
                        scale_ref[row : row + 1, column : column + 1] = scale
                    code_ref[base : base + BLOCK, left : left + BLOCK] = code


def weights_kernel(core_ref, query_ref, other_ref, keyval_ref, smooth_ref, *outs):
    encode(core_ref[0], query_ref, other_ref, keyval_ref, smooth_ref, outs)


def project_kernel(places, core_ref, gathered_ref, smooth_ref, peaks_ref, *refs):
    mine_ref, mine_scale, other_ref, other_scale, out_ref = refs
    members, _, _ = gathered_ref.shape
    depth = smooth_ref.shape[2]
    half = out_ref.shape[1]
    peers = members // 2
    peak = peaks_ref[0]
    for member in range(1, peaks_ref.shape[0]):
        peak = jnp.maximum(peak, peaks_ref[member])
    scale = ((peak + EPSILON) / QSTEPS).astype(jnp.bfloat16).astype(jnp.float32)
    per_block = BLOCK // half
    blocks = depth // BLOCK
    sides = []
    for core, code_ref, scale_ref in (
        (core_ref[0], mine_ref, mine_scale),
        (1 - core_ref[0], other_ref, other_scale),
    ):
        column_scale = [
            jnp.concatenate(
                [
                    jnp.broadcast_to(scale_ref[a : a + 1, c : c + 1], (1, BLOCK))
                    for c in range(scale_ref.shape[1])
                ],
                axis=1,
            )
            for a in range(blocks)
        ]
        sides.append(((1 - core) * peers, smooth_ref[core][1:2, :], code_ref, column_scale))
    for index, first in enumerate(range(0, peers, per_block)):
        row_scale = down(scale[index : index + 1, :])
        row_inverse = 1.0 / row_scale
        total = None
        for start, inverse, code_ref, column_scale in sides:
            for a in range(blocks):
                left = a * BLOCK
                piece = gathered_ref[pl.ds(start + first, per_block), a * half : (a + 1) * half, :]
                piece = piece.astype(jnp.float32).reshape(BLOCK, BLOCK)
                value = piece * inverse[:, left : left + BLOCK] * row_inverse
                code = soften(value).astype(jnp.bfloat16)
                product = jnp.dot(
                    code, code_ref[left : left + BLOCK, :], preferred_element_type=jnp.float32
                )
                product = product * column_scale[a]
                total = product if total is None else total + product
        width = total.shape[1]
        total = jnp.concatenate(
            [total[:, c : c + BLOCK] * row_scale for c in range(0, width, BLOCK)], axis=1
        )
        total = total.astype(out_ref.dtype)
        for peer in range(per_block):
            out_ref[places[first + peer]] = total[peer * half : (peer + 1) * half]


def sum_kernel(parts_ref, out_ref):
    total = parts_ref[0].astype(jnp.float32)
    for part in range(1, parts_ref.shape[0]):
        total = total + parts_ref[part].astype(jnp.float32)
    out_ref[...] = total.astype(out_ref.dtype)


def call(kernel, out_shape, args, **options):
    return launch(kernel, out_shape, args, **options)


def launch(kernel, out_shape, args, flops=0, specs=None, out_specs=None, scratch=()):
    outs = out_shape if isinstance(out_shape, (tuple, list)) else (out_shape,)
    moved = sum(a.size * a.dtype.itemsize for a in (*args, *outs))
    return pl.pallas_call(
        kernel,
        out_shape=out_shape,
        in_specs=specs or [VMEM] * len(args),
        out_specs=out_specs or jax.tree.map(lambda _: VMEM, out_shape),
        scratch_shapes=scratch,
        cost_estimate=pl.CostEstimate(flops=flops, bytes_accessed=moved, transcendentals=0),
        compiler_params=pltpu.CompilerParams(vmem_limit_bytes=8 << 20),
    )(*args)


def exchange(array, axes, order):
    return lax.all_to_all(array, axes, 0, 0, tiled=True, axis_index_groups=[order])


def body(chips, columns, orders, tokens, query_weight, keyval_weight):
    f32, bf16 = jnp.float32, jnp.bfloat16
    shape = jax.ShapeDtypeStruct
    rows, depth = tokens.shape
    half = rows // 2
    width = query_weight.shape[1]
    blocks = depth // BLOCK
    peak_order, part_order, column_order = orders
    core_column_order = [columns + column for column in column_order] + column_order
    places = [part_order.index(column) for column in column_order]
    arguments = (tokens, query_weight, keyval_weight)
    core = lax.axis_index("core").astype(jnp.int32).reshape(1)
    send = call(
        peaks_kernel,
        shape((2 * columns, blocks * (half + 2), BLOCK), bf16),
        (core, *(pltpu.with_memory_space_constraint(a, pltpu.HBM) for a in arguments)),
        specs=[SMEM] + [HBM] * 3,
        out_specs=HBM,
        scratch=[
            *(pltpu.VMEM(a.shape, a.dtype) for a in arguments),
            pltpu.VMEM((2 * columns, blocks * half, BLOCK), bf16),
            pltpu.VMEM((2 * columns, 2 * blocks, BLOCK), bf16),
            pltpu.SemaphoreType.DMA((3,)),
            pltpu.SemaphoreType.DMA((2,)),
        ],
    )
    gathered = exchange(send, ("core", "y", "x"), core_column_order)
    other_weight = lax.ppermute(query_weight, "core", [(0, 1), (1, 0)])
    smooth, row_peaks = call(
        smooth_kernel,
        (shape((2, 8, depth), f32), shape((chips, columns * half // BLOCK, BLOCK), f32)),
        (gathered,),
    )
    peaks = exchange(row_peaks, "z", peak_order)
    code = shape(query_weight.shape, bf16)
    scale = shape((blocks, width // BLOCK), f32)
    query_code, query_scale, *both, keyval_code, keyval_scale = call(
        weights_kernel,
        (
            *(code, scale) * 3,
            shape(keyval_weight.shape, bf16),
            shape((keyval_weight.shape[1] // BLOCK, blocks), f32),
        ),
        (core, query_weight, other_weight, keyval_weight, smooth),
        specs=[SMEM] + [VMEM] * 4,
        flops=20 * (2 * query_weight.size + keyval_weight.size),
    )
    partial = call(
        functools.partial(project_kernel, places),
        shape((chips, half, width), bf16),
        (core, gathered, smooth, peaks, *both),
        specs=[SMEM] + [VMEM] * 7,
        flops=2 * columns * rows * depth * width,
    )
    parts = exchange(partial, "z", part_order)
    query_proj = call(sum_kernel, shape((half, width), bf16), (parts,))
    return (query_proj, query_code, query_scale, keyval_code, keyval_scale.T)


def solution(mesh):
    rows, columns = mesh.devices.shape
    chips = rows // 2
    width = int(round(columns**0.5))
    height = columns // width
    fine = Mesh(mesh.devices.reshape(chips, 2, height, width), ("z", "core", "y", "x"))
    row, col = ("z", "core"), ("y", "x")
    turned = lambda size, first: [(index + first) % size for index in range(size)]
    facing = lambda size, first: [
        (first + index + side * size // 2) % size for index in range(size // 2) for side in range(2)
    ]
    apart = lambda size, first: [
        member for index in range(size - first) for member in (first + index, index)
    ] + [first - 1, size - first]
    orders = (
        facing(chips, 5 * chips // 8),
        apart(chips, chips // 2 + 1),
        [y * width + x for y in turned(height, height - 1) for x in turned(width, width - 1)],
    )
    return jax.shard_map(
        functools.partial(body, chips, columns, orders),
        mesh=fine,
        in_specs=(P(col, row), P(row, col), P(row, col)),
        out_specs=(P(row, col),) * 5,
        check_vma=False,
    )
```

```python
import functools

import jax
import jax.numpy as jnp
from jax import lax
from jax.experimental import pallas as pl
from jax.experimental.pallas import tpu as pltpu
from jax.sharding import Mesh, PartitionSpec as P


BLOCK = 128
QSTEPS = 4
EPSILON = 1e-06
ROUNDER = 12582912.0
SINE = (
    0.8999999761581421,
    -5.921761989593506,
    11.689058303833008,
    -10.986687660217285,
    6.018372535705566,
    -2.1297717094421387,
    0.45832234621047974,
)
VMEM = pl.BlockSpec(memory_space=pltpu.VMEM)
SMEM = pl.BlockSpec(memory_space=pltpu.SMEM)
HBM = pl.BlockSpec(memory_space=pltpu.HBM)


def soften(value):
    offset = value - ((value + ROUNDER) - ROUNDER)
    square = offset * offset
    series = SINE[-1]
    for term in SINE[-2::-1]:
        series = series * square + term
    return value - offset * series


def across(column_major):
    return jnp.max(column_major.T, axis=0, keepdims=True)


def down(row):
    return jnp.broadcast_to(row, (BLOCK, BLOCK)).T


def peaks_kernel(_, tokens_hbm, query_hbm, keyval_hbm, out_hbm, *scratch):
    tokens_ref, query_ref, keyval_ref, rows_ref, both_ref, load_sems, send_sems = scratch
    loads = [
        pltpu.make_async_copy(source, target, load_sems.at[index])
        for index, (source, target) in enumerate(
            ((tokens_hbm, tokens_ref), (query_hbm, query_ref), (keyval_hbm, keyval_ref))
        )
    ]
    for load in loads:
        load.start()
    depth = query_ref.shape[0]
    half = tokens_ref.shape[0] // 2
    body = depth // BLOCK * half
    members = out_hbm.shape[0]
    loads[0].wait()
    for core in range(2):
        for block in range(depth // BLOCK):
            rows = tokens_ref[core * half : (core + 1) * half, block * BLOCK : (block + 1) * BLOCK]
            for peer in range(members // 2):
                rows_ref[(1 - core) * members // 2 + peer, block * half : (block + 1) * half, :] = rows
    sends = [
        pltpu.make_async_copy(rows_ref, out_hbm.at[:, pl.ds(0, body), :], send_sems.at[0]),
        pltpu.make_async_copy(both_ref, out_hbm.at[:, pl.ds(body, both_ref.shape[1]), :], send_sems.at[1]),
    ]
    sends[0].start()
    act = jnp.max(jnp.abs(tokens_ref[...]).astype(jnp.float32), axis=0, keepdims=True)
    acts = [act[:, base : base + BLOCK] for base in range(0, depth, BLOCK)]
    loads[1].wait()
    loads[2].wait()
    peaks = []
    for base in range(0, depth, BLOCK):
        top = jnp.abs(keyval_ref[base : base + BLOCK, :])
        for left in range(0, query_ref.shape[1], BLOCK):
            top = jnp.maximum(top, jnp.abs(query_ref[base : base + BLOCK, left : left + BLOCK]))
        peaks.append(across(top.astype(jnp.float32)))
    both = jnp.concatenate(acts + peaks, axis=0).astype(jnp.bfloat16)
    for member in range(members):
        both_ref[member] = both
    sends[1].start()
    for send in sends:
        send.wait()


def smooth_kernel(gathered_ref, smooth_ref, out_ref):
    members, packed, _ = gathered_ref.shape
    blocks = smooth_ref.shape[2] // BLOCK
    half = packed // blocks - 2
    peers = members // 2
    inverses = []
    for core in range(2):
        both = gathered_ref[(1 - core) * peers, blocks * half :, :]
        for peer in range(1, peers):
            both = jnp.maximum(both, gathered_ref[(1 - core) * peers + peer, blocks * half :, :])
        both = both.astype(jnp.float32)
        smooth = jnp.sqrt((both[:blocks] + EPSILON) / (both[blocks:] + EPSILON))
        inverse = 1.0 / smooth
        for block in range(blocks):
            lanes = slice(block * BLOCK, (block + 1) * BLOCK)
            smooth_ref[core, 0:1, lanes] = smooth[block : block + 1]
            smooth_ref[core, 1:2, lanes] = inverse[block : block + 1]
        inverses.append(inverse)
    per_block = BLOCK // half
    lines = []
    for first in range(0, peers, per_block):
        top = None
        for core in range(2):
            start = (1 - core) * peers + first
            for block in range(blocks):
                rows = slice(block * half, (block + 1) * half)
                piece = jnp.abs(gathered_ref[start : start + per_block, rows, :])
                piece = piece.astype(jnp.float32).reshape(BLOCK, BLOCK)
                piece = piece * inverses[core][block : block + 1]
                top = piece if top is None else jnp.maximum(top, piece)
        lines.append(across(top))
    peak = jnp.concatenate(lines, axis=0)
    for copy in range(out_ref.shape[0]):
        out_ref[copy] = peak


def encode(core, query_ref, other_ref, keyval_ref, smooth_ref, outs):
    query_out, query_scale, mine_out, mine_scale, other_out, other_scale, keyval_out, keyval_scale = outs
    for source, side, targets in (
        (query_ref, core, ((query_out, query_scale), (mine_out, mine_scale))),
        (other_ref, 1 - core, ((other_out, other_scale),)),
        (keyval_ref, core, ((keyval_out, keyval_scale),)),
    ):
        smooth = smooth_ref[side][0:1, :]
        for row, base in enumerate(range(0, source.shape[0], BLOCK)):
            factor = down(smooth[:, base : base + BLOCK])
            for column, left in enumerate(range(0, source.shape[1], BLOCK)):
                block = source[base : base + BLOCK, left : left + BLOCK].astype(jnp.float32) * factor
                top = jnp.max(jnp.max(jnp.abs(block), axis=0, keepdims=True), axis=1, keepdims=True)
                scale = (top + EPSILON) / QSTEPS
                code = soften(block * (1.0 / scale)).astype(jnp.bfloat16)
                for code_ref, scale_ref in targets:
                    if source is keyval_ref:
                        scale_ref[column : column + 1, row : row + 1] = scale
                    else:
                        scale_ref[row : row + 1, column : column + 1] = scale
                    code_ref[base : base + BLOCK, left : left + BLOCK] = code


def weights_kernel(core_ref, query_ref, other_ref, keyval_ref, smooth_ref, *outs):
    encode(core_ref[0], query_ref, other_ref, keyval_ref, smooth_ref, outs)


def project_kernel(places, core_ref, gathered_ref, smooth_ref, peaks_ref, *refs):
    mine_ref, mine_scale, other_ref, other_scale, out_ref = refs
    members, _, _ = gathered_ref.shape
    depth = smooth_ref.shape[2]
    half = out_ref.shape[1]
    peers = members // 2
    peak = peaks_ref[0]
    for member in range(1, peaks_ref.shape[0]):
        peak = jnp.maximum(peak, peaks_ref[member])
    scale = ((peak + EPSILON) / QSTEPS).astype(jnp.bfloat16).astype(jnp.float32)
    per_block = BLOCK // half
    blocks = depth // BLOCK
    sides = []
    for core, code_ref, scale_ref in (
        (core_ref[0], mine_ref, mine_scale),
        (1 - core_ref[0], other_ref, other_scale),
    ):
        column_scale = [
            jnp.concatenate(
                [
                    jnp.broadcast_to(scale_ref[a : a + 1, c : c + 1], (1, BLOCK))
                    for c in range(scale_ref.shape[1])
                ],
                axis=1,
            )
            for a in range(blocks)
        ]
        sides.append(((1 - core) * peers, smooth_ref[core][1:2, :], code_ref, column_scale))
    for index, first in enumerate(range(0, peers, per_block)):
        row_scale = down(scale[index : index + 1, :])
        row_inverse = 1.0 / row_scale
        total = None
        for start, inverse, code_ref, column_scale in sides:
            for a in range(blocks):
                left = a * BLOCK
                piece = gathered_ref[pl.ds(start + first, per_block), a * half : (a + 1) * half, :]
                piece = piece.astype(jnp.float32).reshape(BLOCK, BLOCK)
                value = piece * inverse[:, left : left + BLOCK] * row_inverse
                code = soften(value).astype(jnp.bfloat16)
                product = jnp.dot(
                    code, code_ref[left : left + BLOCK, :], preferred_element_type=jnp.float32
                )
                product = product * column_scale[a]
                total = product if total is None else total + product
        width = total.shape[1]
        total = jnp.concatenate(
            [total[:, c : c + BLOCK] * row_scale for c in range(0, width, BLOCK)], axis=1
        )
        total = total.astype(out_ref.dtype)
        for peer in range(per_block):
            out_ref[places[first + peer]] = total[peer * half : (peer + 1) * half]


def sum_kernel(parts_ref, out_ref):
    total = parts_ref[0].astype(jnp.float32)
    for part in range(1, parts_ref.shape[0]):
        total = total + parts_ref[part].astype(jnp.float32)
    out_ref[...] = total.astype(out_ref.dtype)


def call(kernel, out_shape, args, **options):
    return launch(kernel, out_shape, args, **options)


def launch(kernel, out_shape, args, flops=0, specs=None, out_specs=None, scratch=()):
    outs = out_shape if isinstance(out_shape, (tuple, list)) else (out_shape,)
    moved = sum(a.size * a.dtype.itemsize for a in (*args, *outs))
    return pl.pallas_call(
        kernel,
        out_shape=out_shape,
        in_specs=specs or [VMEM] * len(args),
        out_specs=out_specs or jax.tree.map(lambda _: VMEM, out_shape),
        scratch_shapes=scratch,
        cost_estimate=pl.CostEstimate(flops=flops, bytes_accessed=moved, transcendentals=0),
        compiler_params=pltpu.CompilerParams(vmem_limit_bytes=8 << 20),
    )(*args)


def exchange(array, axes, order):
    return lax.all_to_all(array, axes, 0, 0, tiled=True, axis_index_groups=[order])


def body(chips, columns, orders, tokens, query_weight, keyval_weight):
    f32, bf16 = jnp.float32, jnp.bfloat16
    shape = jax.ShapeDtypeStruct
    rows, depth = tokens.shape
    half = rows // 2
    width = query_weight.shape[1]
    blocks = depth // BLOCK
    peak_order, part_order, column_order = orders
    core_column_order = [columns + column for column in column_order] + column_order
    places = [part_order.index(column) for column in column_order]
    arguments = (tokens, query_weight, keyval_weight)
    core = lax.axis_index("core").astype(jnp.int32).reshape(1)
    send = call(
        peaks_kernel,
        shape((2 * columns, blocks * (half + 2), BLOCK), bf16),
        (core, *(pltpu.with_memory_space_constraint(a, pltpu.HBM) for a in arguments)),
        specs=[SMEM] + [HBM] * 3,
        out_specs=HBM,
        scratch=[
            *(pltpu.VMEM(a.shape, a.dtype) for a in arguments),
            pltpu.VMEM((2 * columns, blocks * half, BLOCK), bf16),
            pltpu.VMEM((2 * columns, 2 * blocks, BLOCK), bf16),
            pltpu.SemaphoreType.DMA((3,)),
            pltpu.SemaphoreType.DMA((2,)),
        ],
    )
    gathered = exchange(send, ("core", "y", "x"), core_column_order)
    other_weight = lax.ppermute(query_weight, "core", [(0, 1), (1, 0)])
    smooth, row_peaks = call(
        smooth_kernel,
        (shape((2, 8, depth), f32), shape((chips, columns * half // BLOCK, BLOCK), f32)),
        (gathered,),
    )
    peaks = exchange(row_peaks, "z", peak_order)
    code = shape(query_weight.shape, bf16)
    scale = shape((blocks, width // BLOCK), f32)
    query_code, query_scale, *both, keyval_code, keyval_scale = call(
        weights_kernel,
        (
            *(code, scale) * 3,
            shape(keyval_weight.shape, bf16),
            shape((keyval_weight.shape[1] // BLOCK, blocks), f32),
        ),
        (core, query_weight, other_weight, keyval_weight, smooth),
        specs=[SMEM] + [VMEM] * 4,
        flops=20 * (2 * query_weight.size + keyval_weight.size),
    )
    partial = call(
        functools.partial(project_kernel, places),
        shape((chips, half, width), bf16),
        (core, gathered, smooth, peaks, *both),
        specs=[SMEM] + [VMEM] * 7,
        flops=2 * columns * rows * depth * width,
    )
    parts = exchange(partial, "z", part_order)
    query_proj = call(sum_kernel, shape((half, width), bf16), (parts,))
    return (query_proj, query_code, query_scale, keyval_code, keyval_scale.T)


def solution(mesh):
    rows, columns = mesh.devices.shape
    chips = rows // 2
    width = int(round(columns**0.5))
    height = columns // width
    fine = Mesh(mesh.devices.reshape(chips, 2, height, width), ("z", "core", "y", "x"))
    row, col = ("z", "core"), ("y", "x")
    turned = lambda size, first: [(index + first) % size for index in range(size)]
    facing = lambda size, first: [
        (first + index + side * size // 2) % size for index in range(size // 2) for side in range(2)
    ]
    orders = (
        facing(chips, 5 * chips // 8),
        facing(chips, chips // 2),
        [y * width + x for y in turned(height, height - 1) for x in turned(width, width - 1)],
    )
    return jax.shard_map(
        functools.partial(body, chips, columns, orders),
        mesh=fine,
        in_specs=(P(col, row), P(row, col), P(row, col)),
        out_specs=(P(row, col),) * 5,
        check_vma=False,
    )
```

```python
import functools

import jax
import jax.numpy as jnp
from jax import lax
from jax.experimental import pallas as pl
from jax.experimental.pallas import tpu as pltpu
from jax.sharding import Mesh, PartitionSpec as P


BLOCK = 128
QSTEPS = 4
EPSILON = 1e-06
ROUNDER = 12582912.0
SINE = (
    0.8999999761581421,
    -5.921761989593506,
    11.689058303833008,
    -10.986687660217285,
    6.018372535705566,
    -2.1297717094421387,
    0.45832234621047974,
)
VMEM = pl.BlockSpec(memory_space=pltpu.VMEM)
SMEM = pl.BlockSpec(memory_space=pltpu.SMEM)
HBM = pl.BlockSpec(memory_space=pltpu.HBM)


def soften(value):
    offset = value - ((value + ROUNDER) - ROUNDER)
    square = offset * offset
    series = SINE[-1]
    for term in SINE[-2::-1]:
        series = series * square + term
    return value - offset * series


def across(column_major):
    return jnp.max(column_major.T, axis=0, keepdims=True)


def down(row):
    return jnp.broadcast_to(row, (BLOCK, BLOCK)).T


def peaks_kernel(_, tokens_hbm, query_hbm, keyval_hbm, out_hbm, *scratch):
    tokens_ref, query_ref, keyval_ref, rows_ref, both_ref, load_sems, send_sems = scratch
    starts = range(0, query_ref.shape[0], BLOCK)
    pairs = [(tokens_hbm, tokens_ref), (keyval_hbm, keyval_ref)]
    pairs += [(query_hbm.at[pl.ds(b, BLOCK), :], query_ref.at[pl.ds(b, BLOCK), :]) for b in starts]
    loads = [
        pltpu.make_async_copy(source, target, load_sems.at[index])
        for index, (source, target) in enumerate(pairs)
    ]
    for load in loads:
        load.start()
    depth = query_ref.shape[0]
    half = tokens_ref.shape[0] // 2
    body = depth // BLOCK * half
    members = out_hbm.shape[0]
    loads[0].wait()
    for core in range(2):
        for block in range(depth // BLOCK):
            rows = tokens_ref[core * half : (core + 1) * half, block * BLOCK : (block + 1) * BLOCK]
            for peer in range(members // 2):
                rows_ref[(1 - core) * members // 2 + peer, block * half : (block + 1) * half, :] = rows
    sends = [
        pltpu.make_async_copy(rows_ref, out_hbm.at[:, pl.ds(0, body), :], send_sems.at[0]),
        pltpu.make_async_copy(both_ref, out_hbm.at[:, pl.ds(body, both_ref.shape[1]), :], send_sems.at[1]),
    ]
    sends[0].start()
    act = jnp.max(jnp.abs(tokens_ref[...]).astype(jnp.float32), axis=0, keepdims=True)
    acts = [act[:, base : base + BLOCK] for base in range(0, depth, BLOCK)]
    loads[1].wait()
    peaks = []
    for base in starts:
        loads[2 + base // BLOCK].wait()
        top = jnp.abs(keyval_ref[base : base + BLOCK, :])
        for left in range(0, query_ref.shape[1], BLOCK):
            top = jnp.maximum(top, jnp.abs(query_ref[base : base + BLOCK, left : left + BLOCK]))
        peaks.append(across(top.astype(jnp.float32)))
    both = jnp.concatenate(acts + peaks, axis=0).astype(jnp.bfloat16)
    for member in range(members):
        both_ref[member] = both
    sends[1].start()
    for send in sends:
        send.wait()


def smooth_kernel(gathered_ref, smooth_ref, out_ref):
    members, packed, _ = gathered_ref.shape
    blocks = smooth_ref.shape[2] // BLOCK
    half = packed // blocks - 2
    peers = members // 2
    inverses = []
    for core in range(2):
        both = gathered_ref[(1 - core) * peers, blocks * half :, :]
        for peer in range(1, peers):
            both = jnp.maximum(both, gathered_ref[(1 - core) * peers + peer, blocks * half :, :])
        both = both.astype(jnp.float32)
        smooth = jnp.sqrt((both[:blocks] + EPSILON) / (both[blocks:] + EPSILON))
        inverse = 1.0 / smooth
        for block in range(blocks):
            lanes = slice(block * BLOCK, (block + 1) * BLOCK)
            smooth_ref[core, 0:1, lanes] = smooth[block : block + 1]
            smooth_ref[core, 1:2, lanes] = inverse[block : block + 1]
        inverses.append(inverse)
    per_block = BLOCK // half
    lines = []
    for first in range(0, peers, per_block):
        top = None
        for core in range(2):
            start = (1 - core) * peers + first
            for block in range(blocks):
                rows = slice(block * half, (block + 1) * half)
                piece = jnp.abs(gathered_ref[start : start + per_block, rows, :])
                piece = piece.astype(jnp.float32).reshape(BLOCK, BLOCK)
                piece = piece * inverses[core][block : block + 1]
                top = piece if top is None else jnp.maximum(top, piece)
        lines.append(across(top))
    peak = jnp.concatenate(lines, axis=0)
    for copy in range(out_ref.shape[0]):
        out_ref[copy] = peak


def encode(core, query_ref, other_ref, keyval_ref, smooth_ref, outs):
    query_out, query_scale, mine_out, mine_scale, other_out, other_scale, keyval_out, keyval_scale = outs
    for source, side, targets in (
        (query_ref, core, ((query_out, query_scale), (mine_out, mine_scale))),
        (other_ref, 1 - core, ((other_out, other_scale),)),
        (keyval_ref, core, ((keyval_out, keyval_scale),)),
    ):
        smooth = smooth_ref[side][0:1, :]
        for row, base in enumerate(range(0, source.shape[0], BLOCK)):
            factor = down(smooth[:, base : base + BLOCK])
            for column, left in enumerate(range(0, source.shape[1], BLOCK)):
                block = source[base : base + BLOCK, left : left + BLOCK].astype(jnp.float32) * factor
                top = jnp.max(jnp.max(jnp.abs(block), axis=0, keepdims=True), axis=1, keepdims=True)
                scale = (top + EPSILON) / QSTEPS
                code = soften(block * (1.0 / scale)).astype(jnp.bfloat16)
                for code_ref, scale_ref in targets:
                    if source is keyval_ref:
                        scale_ref[column : column + 1, row : row + 1] = scale
                    else:
                        scale_ref[row : row + 1, column : column + 1] = scale
                    code_ref[base : base + BLOCK, left : left + BLOCK] = code


def weights_kernel(core_ref, query_ref, other_ref, keyval_ref, smooth_ref, *outs):
    encode(core_ref[0], query_ref, other_ref, keyval_ref, smooth_ref, outs)


def project_kernel(places, core_ref, gathered_ref, smooth_ref, peaks_ref, *refs):
    mine_ref, mine_scale, other_ref, other_scale, out_ref = refs
    members, _, _ = gathered_ref.shape
    depth = smooth_ref.shape[2]
    half = out_ref.shape[1]
    peers = members // 2
    peak = peaks_ref[0]
    for member in range(1, peaks_ref.shape[0]):
        peak = jnp.maximum(peak, peaks_ref[member])
    scale = ((peak + EPSILON) / QSTEPS).astype(jnp.bfloat16).astype(jnp.float32)
    per_block = BLOCK // half
    blocks = depth // BLOCK
    sides = []
    for core, code_ref, scale_ref in (
        (core_ref[0], mine_ref, mine_scale),
        (1 - core_ref[0], other_ref, other_scale),
    ):
        column_scale = [
            jnp.concatenate(
                [
                    jnp.broadcast_to(scale_ref[a : a + 1, c : c + 1], (1, BLOCK))
                    for c in range(scale_ref.shape[1])
                ],
                axis=1,
            )
            for a in range(blocks)
        ]
        sides.append(((1 - core) * peers, smooth_ref[core][1:2, :], code_ref, column_scale))
    for index, first in enumerate(range(0, peers, per_block)):
        row_scale = down(scale[index : index + 1, :])
        row_inverse = 1.0 / row_scale
        total = None
        for start, inverse, code_ref, column_scale in sides:
            for a in range(blocks):
                left = a * BLOCK
                piece = gathered_ref[pl.ds(start + first, per_block), a * half : (a + 1) * half, :]
                piece = piece.astype(jnp.float32).reshape(BLOCK, BLOCK)
                value = piece * inverse[:, left : left + BLOCK] * row_inverse
                code = soften(value).astype(jnp.bfloat16)
                product = jnp.dot(
                    code, code_ref[left : left + BLOCK, :], preferred_element_type=jnp.float32
                )
                product = product * column_scale[a]
                total = product if total is None else total + product
        width = total.shape[1]
        total = jnp.concatenate(
            [total[:, c : c + BLOCK] * row_scale for c in range(0, width, BLOCK)], axis=1
        )
        total = total.astype(out_ref.dtype)
        for peer in range(per_block):
            out_ref[places[first + peer]] = total[peer * half : (peer + 1) * half]


def sum_kernel(parts_ref, out_ref):
    total = parts_ref[0].astype(jnp.float32)
    for part in range(1, parts_ref.shape[0]):
        total = total + parts_ref[part].astype(jnp.float32)
    out_ref[...] = total.astype(out_ref.dtype)


def call(kernel, out_shape, args, **options):
    return launch(kernel, out_shape, args, **options)


def launch(kernel, out_shape, args, flops=0, specs=None, out_specs=None, scratch=()):
    outs = out_shape if isinstance(out_shape, (tuple, list)) else (out_shape,)
    moved = sum(a.size * a.dtype.itemsize for a in (*args, *outs))
    return pl.pallas_call(
        kernel,
        out_shape=out_shape,
        in_specs=specs or [VMEM] * len(args),
        out_specs=out_specs or jax.tree.map(lambda _: VMEM, out_shape),
        scratch_shapes=scratch,
        cost_estimate=pl.CostEstimate(flops=flops, bytes_accessed=moved, transcendentals=0),
        compiler_params=pltpu.CompilerParams(vmem_limit_bytes=8 << 20),
    )(*args)


def exchange(array, axes, order):
    return lax.all_to_all(array, axes, 0, 0, tiled=True, axis_index_groups=[order])


def body(chips, columns, orders, tokens, query_weight, keyval_weight):
    f32, bf16 = jnp.float32, jnp.bfloat16
    shape = jax.ShapeDtypeStruct
    rows, depth = tokens.shape
    half = rows // 2
    width = query_weight.shape[1]
    blocks = depth // BLOCK
    peak_order, part_order, column_order = orders
    core_column_order = [columns + column for column in column_order] + column_order
    places = [part_order.index(column) for column in column_order]
    arguments = (tokens, query_weight, keyval_weight)
    core = lax.axis_index("core").astype(jnp.int32).reshape(1)
    send = call(
        peaks_kernel,
        shape((2 * columns, blocks * (half + 2), BLOCK), bf16),
        (core, *(pltpu.with_memory_space_constraint(a, pltpu.HBM) for a in arguments)),
        specs=[SMEM] + [HBM] * 3,
        out_specs=HBM,
        scratch=[
            *(pltpu.VMEM(a.shape, a.dtype) for a in arguments),
            pltpu.VMEM((2 * columns, blocks * half, BLOCK), bf16),
            pltpu.VMEM((2 * columns, 2 * blocks, BLOCK), bf16),
            pltpu.SemaphoreType.DMA((2 + blocks,)),
            pltpu.SemaphoreType.DMA((2,)),
        ],
    )
    gathered = exchange(send, ("core", "y", "x"), core_column_order)
    other_weight = lax.ppermute(query_weight, "core", [(0, 1), (1, 0)])
    smooth, row_peaks = call(
        smooth_kernel,
        (shape((2, 8, depth), f32), shape((chips, columns * half // BLOCK, BLOCK), f32)),
        (gathered,),
    )
    peaks = exchange(row_peaks, "z", peak_order)
    code = shape(query_weight.shape, bf16)
    scale = shape((blocks, width // BLOCK), f32)
    query_code, query_scale, *both, keyval_code, keyval_scale = call(
        weights_kernel,
        (
            *(code, scale) * 3,
            shape(keyval_weight.shape, bf16),
            shape((keyval_weight.shape[1] // BLOCK, blocks), f32),
        ),
        (core, query_weight, other_weight, keyval_weight, smooth),
        specs=[SMEM] + [VMEM] * 4,
        flops=20 * (2 * query_weight.size + keyval_weight.size),
    )
    partial = call(
        functools.partial(project_kernel, places),
        shape((chips, half, width), bf16),
        (core, gathered, smooth, peaks, *both),
        specs=[SMEM] + [VMEM] * 7,
        flops=2 * columns * rows * depth * width,
    )
    parts = exchange(partial, "z", part_order)
    query_proj = call(sum_kernel, shape((half, width), bf16), (parts,))
    return (query_proj, query_code, query_scale, keyval_code, keyval_scale.T)


def solution(mesh):
    rows, columns = mesh.devices.shape
    chips = rows // 2
    width = int(round(columns**0.5))
    height = columns // width
    fine = Mesh(mesh.devices.reshape(chips, 2, height, width), ("z", "core", "y", "x"))
    row, col = ("z", "core"), ("y", "x")
    turned = lambda size, first: [(index + first) % size for index in range(size)]
    facing = lambda size, first: [
        (first + index + side * size // 2) % size for index in range(size // 2) for side in range(2)
    ]
    apart = lambda size, first: [
        member for index in range(size - first) for member in (first + index, index)
    ] + [first - 1, size - first]
    orders = (
        facing(chips, 5 * chips // 8),
        apart(chips, chips // 2 + 1),
        [y * width + x for y in turned(height, height - 1) for x in turned(width, width - 1)],
    )
    return jax.shard_map(
        functools.partial(body, chips, columns, orders),
        mesh=fine,
        in_specs=(P(col, row), P(row, col), P(row, col)),
        out_specs=(P(row, col),) * 5,
        check_vma=False,
    )
```
